32 devices in a mesh: replica: 8 (over z, core), shard: 4 (over y, x).
Axes of the slice: x: 2, y: 2, z: 4, core: 2. Of those that a mesh axis runs over, the one named last changes fastest.
Arguments:
- tokens: bfloat16 [24576, 768], P(('replica', 'shard')), may hold values from -6 to 6
- cotangent: bfloat16 [24576, 768], P(('replica', 'shard')), may hold values from -6 to 6
- doc_lengths: int32 [32, 4], P(('replica', 'shard')), may hold values from 0 to 768, as said below
- in_weight: bfloat16 [768, 3352], P('shard'), may hold values from -0.21875 to 0.21875
- out_weight: bfloat16 [1536, 768], P('shard'), may hold values from -0.15625 to 0.15625
- conv_weight: bfloat16 [4, 1792], P(None, 'shard'), may hold values from -3 to 3
- conv_bias: bfloat16 [1792], P('shard'), may hold values from -3 to 3
- step_bias: bfloat16 [24], P('shard'), may hold values from -5 to -2
- decay_log: bfloat16 [24], P('shard'), may hold values from 0 to 2.796875
- skip_gain: bfloat16 [24], P('shard'), may hold values from 0.5 to 1.5
- norm_gain: bfloat16 [768], P('shard'), may hold values from 0.5 to 1.5
- gate_gain: bfloat16 [1536], P('shard'), may hold values from 0.5 to 1.5
Outputs:
- layer_out: float32 [24576, 768], P(('replica', 'shard'))
- input_grad: float32 [24576, 768], P(('replica', 'shard'))
- in_weight_grad: float32 [768, 3352], P('shard')
- out_weight_grad: float32 [1536, 768], P('shard')
- conv_weight_grad: float32 [4, 1792], P(None, 'shard')
- conv_bias_grad: float32 [1792], P('shard')
- step_bias_grad: float32 [24], P('shard')
- decay_log_grad: float32 [24], P('shard')
- skip_gain_grad: float32 [24], P('shard')
- norm_gain_grad: float32 [768], P('shard')
- gate_gain_grad: float32 [1536], P('shard')
The draws below stay inside these ranges and needn't reach their ends.
Inputs may be any that keep to these rules, and one draw needn't show every extreme that they name: `doc_lengths`: row k lists the lengths of the sequences packed in order from the start of device block k; a zero is an empty entry; every row sums to at most 768, and some row is one sequence of 768 slots.
All inputs are finite; a program needn't handle non-finite values.
Results may differ from the reference program's by a relative error of at most 0.0071.
Values may be sent and summed in bfloat16 or wider, within the bound.
A program may use at most 256 MiB of HBM per device.

```python
import jax
import jax.numpy as jnp
from jax import lax

D = 768
HEADS = 24
KERNEL = 4
BLOCK = 256
TOK_DEV = 768
SLOTS = 4
INNER = 1536
CONVD = 1792
PROJ = 3352
TOKENS = 24576
N_REPLICA = 8
N_SHARD = 4


def draw_doc_lengths(key, part):
    devices_all = N_REPLICA * N_SHARD
    subkeys = jax.random.split(jax.random.fold_in(key, 17), 3)
    fills = jax.random.randint(subkeys[0], (devices_all,), TOK_DEV // 4, TOK_DEV + 1).astype(jnp.int32)
    cuts = jnp.sort(jax.random.randint(subkeys[1], (devices_all, SLOTS - 1), 0, TOK_DEV + 1).astype(jnp.int32), axis=1)
    scaled = cuts * fills[:, None] // TOK_DEV
    bounds = jnp.concatenate([jnp.zeros((devices_all, 1), jnp.int32), scaled, fills[:, None]], axis=1)
    lengths = bounds[:, 1:] - bounds[:, :-1]
    chosen = jax.random.randint(subkeys[2], (), 0, devices_all).astype(jnp.int32)
    single = jnp.concatenate([jnp.full((1,), TOK_DEV, jnp.int32), jnp.zeros((SLOTS - 1,), jnp.int32)])
    rows_index = jnp.arange(devices_all, dtype=jnp.int32)
    lengths = jnp.where((rows_index == chosen)[:, None], single[None, :], lengths)
    return lengths.astype(jnp.int32)


def block_levels(stream_key, dims, cuts, least, high):
    gain = 1.0
    for dim, blocks in cuts:
        draws = jax.random.uniform(jax.random.fold_in(jax.random.fold_in(stream_key, 6), dim), (blocks,), jnp.float32, least / len(cuts), high / len(cuts))
        gain = gain * jnp.repeat(jnp.exp(draws), dims[dim] // blocks).reshape((-1,) + (1,) * (len(dims) - 1 - dim))
    return gain


def centred(stream_key, extent, width, bound, cuts=(), held_as=jnp.bfloat16):
    loudness = block_levels(stream_key, extent, cuts, -0.22, 0.18) if cuts else 1.0
    entries = jax.random.normal(stream_key, extent, jnp.float32) * width * loudness
    return jnp.minimum(jnp.maximum(entries, -bound), bound).astype(held_as)


def setup_inputs(seed: int = 0) -> dict:
    key_list = jax.random.split(jax.random.key(seed), 13)
    return {
        "tokens": centred(key_list[0], (TOKENS, D), 1.0, 6.0, ((0, 32),)),
        "cotangent": centred(key_list[1], (TOKENS, D), 1.0, 6.0, ((0, 32),)),
        "doc_lengths": draw_doc_lengths(jax.random.fold_in(key_list[12], 71), 0),
        "in_weight": centred(key_list[3], (D, PROJ), D ** -0.5, 0.21875, ((0, 4),)),
        "out_weight": centred(key_list[4], (INNER, D), INNER ** -0.5, 0.15625, ((0, 4),)),
        "conv_weight": centred(key_list[5], (KERNEL, CONVD), KERNEL ** -0.5, 3.0, ((1, 4),)),
        "conv_bias": centred(key_list[6], (CONVD,), 0.5, 3.0, ((0, 4),)),
        "step_bias": jnp.clip(-5.0 + 3.0 * jax.random.uniform(key_list[7], (HEADS,), jnp.float32) ** block_levels(key_list[7], (HEADS,), ((0, 4),), -0.2, 0.2), -5.0, -2.0).astype(jnp.bfloat16),
        "decay_log": jnp.clip(2.796875 * jax.random.uniform(key_list[8], (HEADS,), jnp.float32) ** block_levels(key_list[8], (HEADS,), ((0, 4),), -0.2, 0.2), 0.0, 2.796875).astype(jnp.bfloat16),
        "skip_gain": jnp.clip(0.5 + 1.0 * jax.random.uniform(key_list[9], (HEADS,), jnp.float32) ** block_levels(key_list[9], (HEADS,), ((0, 4),), -0.2, 0.2), 0.5, 1.5).astype(jnp.bfloat16),
        "norm_gain": jnp.clip(1.0 + 0.1 * jax.random.normal(key_list[10], (D,), jnp.float32), 0.5, 1.5).astype(jnp.bfloat16),
        "gate_gain": jnp.clip(1.0 + 0.1 * jax.random.normal(key_list[11], (INNER,), jnp.float32), 0.5, 1.5).astype(jnp.bfloat16),
    }


EPS = 1e-05
HIGH = lax.Precision.HIGHEST

def prenorm(values, gain_vec):
    scales = lax.rsqrt(lax.optimization_barrier(jnp.mean(values * values, axis=1, keepdims=True)) + EPS)
    return values * scales * gain_vec[None, :]

def segments_of(lengths, length):
    boundary = jnp.cumsum(lengths).astype(jnp.int32)
    places = jnp.arange(length, dtype=jnp.int32)
    segment = lax.optimization_barrier(jnp.sum((places[:, None] >= boundary[None, :]).astype(jnp.int32), axis=1)).astype(jnp.int32)
    return (segment, places < boundary[-1])

def conv_causal(values, segment, kernel_taps, bias_row):
    kernel_len = kernel_taps.shape[0]
    result = bias_row[None, :] + kernel_taps[kernel_len - 1][None, :] * values
    for offset in range(1, kernel_len):
        shifted = jnp.concatenate([jnp.zeros((offset, values.shape[1]), values.dtype), values[:-offset]], axis=0)
        earlier = jnp.concatenate([jnp.full((offset,), -1, jnp.int32), segment[:-offset]], axis=0)
        result = result + kernel_taps[kernel_len - 1 - offset][None, :] * jnp.where((earlier == segment)[:, None], shifted, 0.0)
    return result

def scan_blocks(inputs, spacing, decays, key_rows, query_rows, segment, block_len):
    length, head_count, head_width = inputs.shape
    block_count = length // block_len
    state_size = key_rows.shape[1]
    places = jnp.arange(block_len, dtype=jnp.int32)
    lower_tri = places[:, None] >= places[None, :]
    inputs_b = inputs.reshape(block_count, block_len, head_count, head_width)
    spacing_b = spacing.reshape(block_count, block_len, head_count)
    keys_b = key_rows.reshape(block_count, block_len, state_size)
    queries_b = query_rows.reshape(block_count, block_len, state_size)
    segment_b = segment.reshape(block_count, block_len)
    cumulated = jnp.cumsum(spacing_b * decays[None, None, :], axis=1)
    same_seg = (segment_b[:, :, None] == segment_b[:, None, :]) & lower_tri[None]
    by_head = jnp.swapaxes(cumulated, 1, 2)
    spread = by_head[:, :, :, None] - by_head[:, :, None, :]
    within = jnp.where(same_seg[:, None], jnp.exp(jnp.where(same_seg[:, None], spread, 0.0)), 0.0)
    gram_mat = jnp.einsum('bin,bjn->bij', queries_b, keys_b, precision=HIGH)
    mixing = within * gram_mat[:, None] * jnp.swapaxes(spacing_b, 1, 2)[:, :, None, :]
    inside = jnp.einsum('bhij,bjhp->bihp', mixing, inputs_b, precision=HIGH)
    final_seg = segment_b[:, block_len - 1]
    before = jnp.concatenate([jnp.full((1,), -1, jnp.int32), final_seg[:-1]], axis=0)
    end_decay = cumulated[:, block_len - 1]
    ending = jnp.where((segment_b == final_seg[:, None])[:, :, None], jnp.exp(end_decay[:, None, :] - cumulated), 0.0) * spacing_b
    retained = jnp.where((final_seg == before)[:, None], jnp.exp(end_decay), 0.0)
    injected = jnp.einsum('bjh,bjhp,bjn->bhpn', ending, inputs_b, keys_b, precision=HIGH)

    def advance(states, pieces):
        kept, added = pieces
        return (kept[:, None, None] * states + added, states)
    initial = jnp.zeros((head_count, head_width, state_size), jnp.float32)
    _, starts = lax.scan(advance, initial, (retained, injected))
    carry_rows = (segment_b == before[:, None]).astype(jnp.float32)[:, :, None] * jnp.exp(cumulated)
    incoming = jnp.einsum('bin,bhpn->bihp', queries_b, starts, precision=HIGH) * carry_rows[:, :, :, None]
    return (inside + incoming).reshape(length, head_count, head_width)

def mixer(projected, segment, kernel_taps, bias_row, step_shift, decay_logs, skip_row, gate_row):
    length = projected.shape[0]
    inner = gate_row.shape[0]
    head_count = step_shift.shape[0]
    channels = kernel_taps.shape[1]
    state_size = (channels - inner) // 2
    gate_rows = projected[:, :inner]
    conv_in = projected[:, inner:inner + channels]
    step_raw = projected[:, inner + channels:]
    conv_out = jax.nn.silu(conv_causal(conv_in, segment, kernel_taps, bias_row))
    inputs = conv_out[:, :inner].reshape(length, head_count, inner // head_count)
    key_rows = conv_out[:, inner:inner + state_size]
    query_rows = conv_out[:, inner + state_size:]
    spacing = jax.nn.softplus(step_raw + step_shift[None, :])
    decays = -jnp.exp(decay_logs)
    outputs = scan_blocks(inputs, spacing, decays, key_rows, query_rows, segment, BLOCK)
    outputs = outputs + skip_row[None, :, None] * inputs
    gated = outputs.reshape(length, inner) * jax.nn.silu(gate_rows)
    return prenorm(gated, gate_row)

def device_pass(tokens, cotangent, lengths, params):
    segment, valid = segments_of(lengths, tokens.shape[0])
    in_full, out_full = (params[0], params[1])
    smalls = tuple((piece.astype(jnp.float32) for piece in (params[2], params[3], params[4], params[5], params[6], params[8])))
    gain_vec = params[7].astype(jnp.float32)
    values = tokens.astype(jnp.float32)
    normed = prenorm(values, gain_vec).astype(jnp.bfloat16)
    projected = jnp.dot(normed, in_full, preferred_element_type=jnp.float32)

    def apply_mixer(proj_in, taps, bias_row, shift, logs, skip_row, gate_row):
        return mixer(proj_in, segment, taps, bias_row, shift, logs, skip_row, gate_row)
    mixed, mixer_back = jax.vjp(apply_mixer, projected, *smalls)
    mixed_b = mixed.astype(jnp.bfloat16)
    valid_col = valid.astype(jnp.float32)[:, None]
    layer = values + valid_col * jnp.dot(mixed_b, out_full, preferred_element_type=jnp.float32)
    masked = cotangent * valid.astype(jnp.bfloat16)[:, None]
    grad_outw = lax.dot_general(mixed_b, masked, (((0,), (0,)), ((), ())), preferred_element_type=jnp.float32)
    grad_mixed = lax.dot_general(masked, out_full, (((1,), (1,)), ((), ())), preferred_element_type=jnp.float32)
    mixer_grads = mixer_back(grad_mixed)
    grad_projected = mixer_grads[0]
    grad_proj = grad_projected.astype(jnp.bfloat16)
    grad_inw = lax.dot_general(normed, grad_proj, (((0,), (0,)), ((), ())), preferred_element_type=jnp.float32)
    grad_normed = lax.dot_general(grad_proj, in_full, (((1,), (1,)), ((), ())), preferred_element_type=jnp.float32)
    _, norm_back = jax.vjp(prenorm, values, gain_vec)
    grad_norm_in, grad_gain = norm_back(grad_normed)
    input_grad = cotangent.astype(jnp.float32) + grad_norm_in
    grads = (grad_inw, grad_outw, mixer_grads[1], mixer_grads[2], mixer_grads[3], mixer_grads[4], mixer_grads[5], grad_gain, mixer_grads[6])
    return (layer, input_grad, grads)

def reference(tokens, cotangent, doc_lengths, in_weight, out_weight, conv_weight, conv_bias, step_bias, decay_log, skip_gain, norm_gain, gate_gain):
    devices_all = N_REPLICA * N_SHARD
    params = (in_weight, out_weight, conv_weight, conv_bias, step_bias, decay_log, skip_gain, norm_gain, gate_gain)
    blocks_in = tokens.reshape(devices_all, TOK_DEV, D)
    blocks_cot = cotangent.reshape(devices_all, TOK_DEV, D)
    zeros_all = tuple((jnp.zeros(piece.shape, jnp.float32) for piece in params))

    def per_device(totals, pieces):
        layer, input_grad, grads = device_pass(pieces[0], pieces[1], pieces[2], params)
        return (tuple((first + second for first, second in zip(totals, grads))), (layer, input_grad))
    totals, (layers, inputs_grad) = lax.scan(per_device, zeros_all, (blocks_in, blocks_cot, doc_lengths))
    return (layers.reshape(TOKENS, D), inputs_grad.reshape(TOKENS, D), totals[0], totals[1], totals[2], totals[3], totals[4], totals[5], totals[6], totals[7], totals[8])
```

```python
import functools

import jax
import jax.numpy as jnp
from jax import lax
from jax.experimental import pallas as pl
from jax.experimental.pallas import tpu as pltpu
from jax.sharding import PartitionSpec as P

BLOCK = 256
LANES = 128
EPS = 1e-05
HIGH = lax.Precision.HIGHEST
BF = jnp.bfloat16
F32 = jnp.float32


def dot(a, b, dims=((1,), (0,)), precision=None):
    return lax.dot_general(a, b, (dims, ((), ())), preferred_element_type=F32, precision=precision)


def split(v):
    hi = v.astype(BF)
    return hi, (v - hi.astype(F32)).astype(BF)


def dot_split(mix_hi, mix_lo, v, dims):
    hi, lo = split(v)
    width = v.shape[1]
    both = dot(mix_hi, jnp.concatenate([hi, lo], axis=1), dims)
    return both[:, :width] + both[:, width:] + dot(mix_lo, hi, dims)


def prenorm(values, gain_vec):
    scales = lax.rsqrt(jnp.mean(values * values, axis=1, keepdims=True) + EPS)
    return values * scales * gain_vec[None, :]


def segments_of(lengths, length):
    boundary = jnp.cumsum(lengths)
    places = jnp.arange(length, dtype=jnp.int32)
    segment = jnp.sum((places[:, None] >= boundary[None, :]).astype(jnp.int32), axis=1)
    return (segment, places < boundary[-1])


def conv_causal(values, masks, kernel_taps, bias_row):
    kernel_len = kernel_taps.shape[0]
    result = bias_row[None, :] + kernel_taps[kernel_len - 1][None, :] * values
    for offset in range(1, kernel_len):
        shifted = jnp.concatenate(
            [jnp.zeros((offset, values.shape[1]), values.dtype), values[:-offset]], axis=0
        )
        result = result + kernel_taps[kernel_len - 1 - offset][None, :] * jnp.where(
            masks[offset - 1][:, None], shifted, 0.0
        )
    return result


def mixer_kernel(
    inner, taps_n, block, width,
    z_ref, cin_ref, gm_ref, par_ref, mask_ref, gram_ref,
    rows_ref, cols_ref, fac_ref,
    dz_ref, dcin_ref, mixed_ref, dgram_ref, dc_ref, ddt_ref, sums_ref,
    pre_s, u_s, yd_s, yo_s, mix_s, low_s, ss_s, q_s,
):
    phase, g = pl.program_id(0), pl.program_id(1)
    taps_ref = par_ref.at[0:4]
    bias_ref, gain_ref, skip_ref = par_ref.at[4:5], par_ref.at[5:6], par_ref.at[7:8]
    length = z_ref.shape[0]
    nb = length // block
    heads = LANES // width

    def col(k, rows):
        parts = [
            jnp.broadcast_to(cols_ref[0, rows, k * heads + h : k * heads + h + 1], (block, width))
            for h in range(heads)
        ]
        return jnp.concatenate(parts, axis=1)

    def shifted_in(k):
        return pltpu.roll(cin_ref[...], k, 0) * mask_ref[k - 1]

    blocks = [slice(i * block, (i + 1) * block) for i in range(nb)]

    @pl.when((phase == 0) & (g == 0))
    def _():
        ss_s[...] = jnp.zeros_like(ss_s)
        q_s[...] = jnp.zeros_like(q_s)
        dgram_ref[...] = jnp.zeros_like(dgram_ref)
        dc_ref[...] = jnp.zeros_like(dc_ref)
        ddt_ref[...] = jnp.zeros_like(ddt_ref)

    @pl.when(phase == 0)
    def _():
        pre = bias_ref[0:1, :] + taps_ref[taps_n - 1 : taps_n, :] * cin_ref[...]
        for k in range(1, taps_n):
            pre = pre + taps_ref[taps_n - 1 - k : taps_n - k, :] * shifted_in(k)
        pre_s[g] = pre
        vs = []
        for i in range(nb):
            r = blocks[i]
            p_r = pre_s[g, r, :]
            x = p_r * jax.nn.sigmoid(p_r)
            u = x * col(1, r)
            u_s[g, r, :] = u
            vs.append((u * col(3, r)).astype(BF))
            ys = []
            for h in range(heads):
                spread = cols_ref[0, r, h : h + 1] - rows_ref[0, h : h + 1, r]
                hi, lo = split(jnp.exp(jnp.minimum(spread, 0.0)) * gram_ref[r, r])
                mix_s[g, h, i] = hi
                low_s[g, h, i] = lo
                ys.append(dot_split(hi, lo, u[:, h * width : (h + 1) * width], ((1,), (0,))))
            yd = jnp.concatenate(ys, axis=1)
            yd_s[g, r, :] = yd
            yo = jnp.zeros((block, LANES), F32)
            for j in range(i):
                yo = yo + dot(gram_ref[r, blocks[j]].astype(BF), vs[j]) * fac_ref[i * nb + j : i * nb + j + 1, :]
            yo_s[g, r, :] = yo
            z = z_ref[r, :]
            gated = (yd + yo * col(2, r) + skip_ref[0:1, :] * x) * (z * jax.nn.sigmoid(z))
            ss_s[r, :] += gated * gated
            q_s[r, :] += gm_ref[r, :] * gain_ref[0:1, :] * gated

    @pl.when((phase == 1) & (g == 0))
    def _():
        scale = lax.rsqrt(jnp.sum(ss_s[...], axis=1, keepdims=True) / inner + EPS)
        coef = jnp.sum(q_s[...], axis=1, keepdims=True) * scale * scale * scale / inner
        ss_s[...] = jnp.broadcast_to(scale, ss_s.shape)
        q_s[...] = jnp.broadcast_to(coef, q_s.shape)

    @pl.when(phase == 1)
    def _():
        lane = lax.broadcasted_iota(jnp.int32, (LANES, LANES), 0) // width
        target = lax.broadcasted_iota(jnp.int32, (LANES, LANES), 1)
        pick = jnp.where(lane + g * heads == target, 1.0, 0.0).astype(BF)

        def by_head(d):
            hi = d.astype(BF)
            lo = (d - hi.astype(F32)).astype(BF)
            return dot(hi, pick) + dot(lo, pick)

        dys_all, ws, vs = [], [], []
        dskip = jnp.zeros((1, LANES), F32)
        dgain = jnp.zeros((1, LANES), F32)
        for i in range(nb):
            r = blocks[i]
            p_r = pre_s[g, r, :]
            x = p_r * jax.nn.sigmoid(p_r)
            z = z_ref[r, :]
            sig = jax.nn.sigmoid(z)
            act = z * sig
            a = col(2, r)
            y = yd_s[g, r, :] + yo_s[g, r, :] * a + skip_ref[0:1, :] * x
            gated = y * act
            scale = ss_s[r, :]
            mixed_ref[r, :] = (gated * scale * gain_ref[0:1, :]).astype(BF)
            gm = gm_ref[r, :]
            dgain = dgain + jnp.sum(gm * gated * scale, axis=0, keepdims=True)
            dgated = gm * gain_ref[0:1, :] * scale - gated * q_s[r, :]
            dz_ref[r, :] = (dgated * y * (sig + act * (1.0 - sig))).astype(BF)
            dy = dgated * act
            dskip = dskip + jnp.sum(dy * x, axis=0, keepdims=True)
            dys_all.append(dy)
            ws.append((dy * a).astype(BF))
            vs.append((u_s[g, r, :] * col(3, r)).astype(BF))
        for j in range(nb):
            r = blocks[j]
            dy = dys_all[j]
            dyb = dy.astype(BF)
            u = u_s[g, r, :]
            ub = u.astype(BF)
            dus = []
            dgram = jnp.zeros((block, block), F32)
            for h in range(heads):
                lanes = slice(h * width, (h + 1) * width)
                dus.append(dot_split(mix_s[g, h, j], low_s[g, h, j], dy[:, lanes], ((0,), (0,))))
                spread = cols_ref[0, r, h : h + 1] - rows_ref[0, h : h + 1, r]
                decay = jnp.exp(jnp.minimum(spread, 0.0))
                dgram = dgram + decay * dot(dyb[:, lanes], ub[:, lanes], ((1,), (1,)))
            dgram_ref[r, r] += dgram
            du = jnp.concatenate(dus, axis=1)
            dv = jnp.zeros((block, LANES), F32)
            for i in range(j + 1, nb):
                fac = fac_ref[i * nb + j : i * nb + j + 1, :]
                dv = dv + dot(gram_ref[blocks[i], r].astype(BF), ws[i], ((0,), (0,))) * fac
                dgram_ref[blocks[i], r] += dot(
                    (ws[i].astype(F32) * fac).astype(BF), vs[j], ((1,), (1,))
                )
            dc_ref[r, :] += by_head(
                dy * yd_s[g, r, :]
                + ws[j].astype(F32) * yo_s[g, r, :]
                - u * du
                - vs[j].astype(F32) * dv
            )
            du = du + dv * col(3, r)
            p_r = pre_s[g, r, :]
            sig = jax.nn.sigmoid(p_r)
            x = p_r * sig
            ddt_ref[r, :] += by_head(du * x)
            dx = skip_ref[0:1, :] * dy + du * col(1, r)
            yd_s[g, r, :] = dx * (sig + x * (1.0 - sig))
        dpre = yd_s[g]
        dcin = taps_ref[taps_n - 1 : taps_n, :] * dpre
        sums_ref[taps_n - 1 : taps_n, :] = jnp.sum(dpre * cin_ref[...], axis=0, keepdims=True)
        for k in range(1, taps_n):
            masked = dpre * mask_ref[k - 1]
            dcin = dcin + taps_ref[taps_n - 1 - k : taps_n - k, :] * pltpu.roll(masked, length - k, 0)
            sums_ref[taps_n - 1 - k : taps_n - k, :] = jnp.sum(
                masked * pltpu.roll(cin_ref[...], k, 0), axis=0, keepdims=True
            )
        dcin_ref[...] = dcin.astype(BF)
        sums_ref[taps_n : taps_n + 1, :] = jnp.sum(dpre, axis=0, keepdims=True)
        sums_ref[taps_n + 2 : taps_n + 3, :] = dskip
        sums_ref[taps_n + 1 : taps_n + 2, :] = dgain
        sums_ref[taps_n + 3 : taps_n + 4, :] = jnp.zeros((1, LANES), F32)


def mixer_call(projected, gm, par, inner, taps_n, conv_masks, gram, spacing, cum, heads_all):
    length = projected.shape[0]
    width = inner // heads_all
    heads = LANES // width
    groups = inner // LANES
    block = BLOCK
    nb = length // block
    ends = cum[block - 1 :: block]
    starts = jnp.concatenate([jnp.zeros((1, heads_all), F32), ends[:-1]], axis=0)
    cum_b = cum.reshape(nb, block, heads_all)
    enter = jnp.exp(cum_b - starts[:, None]).reshape(length, heads_all)
    leave = jnp.exp(ends[:, None] - cum_b).reshape(length, heads_all)
    fac = jnp.exp(jnp.minimum(starts[:, None] - ends[None, :], 0.0)).reshape(nb * nb, heads_all)
    fac = jnp.repeat(fac, width, axis=1)
    cols = jnp.stack([cum, spacing, enter, leave], axis=1).reshape(length, 4, groups, heads)
    cols = cols.transpose(2, 0, 1, 3).reshape(groups, length, 4 * heads)
    rows = cum.T.reshape(groups, heads, length)
    wide = lambda m: jnp.broadcast_to(m[:, None], (length, LANES)).astype(F32)
    masks = jnp.stack([wide(m) for m in conv_masks])
    n_sum = 8

    part = lambda off: pl.BlockSpec((length, LANES), lambda p, g: (0, off + g))
    row = lambda n: pl.BlockSpec((n, LANES), lambda p, g: (0, g))
    full = lambda *s: pl.BlockSpec(s, lambda p, g: (0,) * len(s))
    late = lambda n: pl.BlockSpec((n, LANES), lambda p, g: (0, p * g))
    sds = jax.ShapeDtypeStruct
    return pl.pallas_call(
        functools.partial(mixer_kernel, inner, taps_n, block, width),
        grid=(2, groups),
        in_specs=[
            part(0), part(groups), part(0), row(8),
            full(taps_n - 1, length, LANES), full(length, length),
            pl.BlockSpec((1, heads, length), lambda p, g: (g, 0, 0)),
            pl.BlockSpec((1, length, 4 * heads), lambda p, g: (g, 0, 0)),
            row(nb * nb),
        ],
        out_specs=[
            late(length), late(length), late(length), full(length, length),
            full(length, LANES), full(length, LANES), late(n_sum),
        ],
        out_shape=[
            sds((length, inner), BF), sds((length, inner), BF), sds((length, inner), BF),
            sds((length, length), F32), sds((length, LANES), F32), sds((length, LANES), F32),
            sds((n_sum, inner), F32),
        ],
        scratch_shapes=[
            pltpu.VMEM((groups, length, LANES), F32),
            pltpu.VMEM((groups, length, LANES), F32),
            pltpu.VMEM((groups, length, LANES), F32),
            pltpu.VMEM((groups, length, LANES), F32),
            pltpu.VMEM((groups, heads, nb, block, block), BF),
            pltpu.VMEM((groups, heads, nb, block, block), BF),
            pltpu.VMEM((length, LANES), F32),
            pltpu.VMEM((length, LANES), F32),
        ],
        compiler_params=pltpu.CompilerParams(
            vmem_limit_bytes=60 * 1024 * 1024, dimension_semantics=("arbitrary", "arbitrary")
        ),
        cost_estimate=pl.CostEstimate(
            flops=20 * length * block * inner, bytes_accessed=40 * length * inner, transcendentals=0
        ),
    )(
        projected, projected, gm, par, masks, gram, rows, cols, fac,
    )


def device_part(tokens, cotangent, lengths, in_full, out_full, par, head, n, dims):
    cw, gw, nw, hw = dims
    length = tokens.shape[0]
    segment, valid = segments_of(lengths, length)
    inner, channels, heads_all = n * gw, n * cw, n * hw
    taps, bias = par[0:4, :channels], par[4, :channels]
    step_bias, decay_log = head[0, :heads_all], head[1, :heads_all]
    gain_vec = par[6, : n * nw]
    state = (channels - inner) // 2
    values = tokens.astype(F32)
    normed = prenorm(values, gain_vec).astype(BF)
    projected = dot(normed, in_full)
    masked = cotangent * valid.astype(BF)[:, None]
    grad_mixed = dot(masked, out_full, ((1,), (1,)))
    places = jnp.arange(length, dtype=jnp.int32)
    lower = places[:, None] >= places[None, :]
    conv_masks = [
        (places >= k) & (jnp.roll(segment, k) == segment) for k in range(1, taps.shape[0])
    ]
    same = lower & (segment[:, None] == segment[None, :])

    def gram_of(cin, taps_bc, bias_bc):
        out = jax.nn.silu(conv_causal(cin, conv_masks, taps_bc, bias_bc))
        return jnp.where(same, dot(out[:, state:], out[:, :state], ((1,), (1,)), HIGH), 0.0)

    def steps_of(raw, shift, logs):
        spacing = jax.nn.softplus(raw + shift[None, :])
        cum = dot(lower.astype(F32), spacing * -jnp.exp(logs)[None, :], precision=HIGH)
        return spacing, cum

    gram, gram_back = jax.vjp(
        gram_of, projected[:, 2 * inner : inner + channels], taps[:, inner:], bias[inner:]
    )
    (spacing, cum), steps_back = jax.vjp(
        steps_of, projected[:, inner + channels :], step_bias, decay_log
    )
    dz, dcin, mixed, dgram, dcum, dspacing, sums = mixer_call(
        projected, grad_mixed, par, inner, taps.shape[0], conv_masks, gram, spacing, cum, heads_all
    )
    d_bc, dtaps_bc, dbias_bc = gram_back(dgram)
    d_raw, d_shift, d_logs = steps_back((dspacing[:, :heads_all], dcum[:, :heads_all]))
    d_skip = jnp.sum(sums[6].reshape(heads_all, -1), axis=1)
    grad_proj = jnp.concatenate([dz, dcin, d_bc.astype(BF), d_raw.astype(BF)], axis=1)
    layer = values + valid.astype(F32)[:, None] * dot(mixed, out_full)
    grad_outw = dot(mixed, masked, ((0,), (0,)))
    grad_inw = dot(normed, grad_proj, ((0,), (0,)))
    grad_normed = dot(grad_proj, in_full, ((1,), (1,)))
    _, norm_back = jax.vjp(prenorm, values, gain_vec)
    grad_norm_in, grad_gain = norm_back(grad_normed)
    input_grad = cotangent.astype(F32) + grad_norm_in
    fit = lambda v, w: jnp.pad(v, ((0, 0), (0, w - v.shape[1])))
    dpar = jnp.concatenate([
        jnp.concatenate([sums[:5], jnp.concatenate([dtaps_bc, dbias_bc[None]])], axis=1),
        fit(sums[5:6], channels), fit(grad_gain[None], channels), jnp.zeros((1, channels), F32),
    ])
    dhead = jnp.pad(jnp.stack([d_shift, d_logs, d_skip]), ((0, 5), (0, LANES - heads_all)))
    return layer, input_grad, grad_inw, grad_outw, dpar, dhead


def moved(x, step):
    n_rep, n = lax.axis_size("replica"), lax.axis_size("shard")
    perm = []
    for r in range(n_rep):
        for s in range(n):
            to_r, to_s = step(r, s)
            perm.append((r * n + s, to_r * n + to_s))
    return lax.ppermute(x, ("replica", "shard"), perm)


def pick(x, i):
    return lax.dynamic_index_in_dim(x, i, 0, keepdims=False)


def ring_all(x, index, n, step):
    got = jnp.stack([x] + [moved(x, functools.partial(step, k)) for k in range(1, n)])
    return jnp.stack([pick(got, lax.rem(index - j + n, n)) for j in range(n)])


def ring_sum(parts, index, n, step):
    total = pick(parts, index).astype(F32)
    for k in range(1, n):
        total = total + moved(pick(parts, lax.rem(index + k, n)), functools.partial(step, k))
    return total


def shard_step(k, r, s):
    return r, (s + k) % lax.axis_size("shard")


def chip_step(k, r, s):
    return (r + 2 * k) % lax.axis_size("replica"), s


def core_step(r, s):
    return r ^ 1, s


def both_halves(mine, core, axis):
    other = moved(mine, core_step)
    first = jnp.where(core == 0, mine, other)
    second = jnp.where(core == 0, other, mine)
    return jnp.stack([first, second], axis=axis)


def gather_weight(shard, core, me, n):
    half = pick(shard.reshape(2, -1, shard.shape[1]), core)
    mine = ring_all(half, me, n, shard_step)
    return both_halves(mine, core, 1).reshape(-1, shard.shape[1])


def reduce_grad(grad, core, me, n, chip, chips, kind):
    columns = grad.shape[1]
    blocks = grad.astype(kind).reshape(n, 2, -1, columns)
    keep = lax.dynamic_index_in_dim(blocks, core, 1, keepdims=False)
    send = lax.dynamic_index_in_dim(blocks, 1 - core, 1, keepdims=False)
    pair = (keep.astype(F32) + moved(send, core_step).astype(F32)).astype(kind)
    mine = ring_sum(pair, me, n, shard_step).astype(kind)
    piece = ring_sum(mine.reshape(chips, -1, columns), chip, chips, chip_step).astype(kind)
    half = ring_all(piece, chip, chips, chip_step).reshape(-1, columns)
    return both_halves(half, core, 0).reshape(-1, columns).astype(F32)


MESH = pl.DeviceIdType.MESH


def peers():
    rep, s = lax.axis_index("replica"), lax.axis_index("shard")
    return rep, s


def flip(v, bit):
    return v + bit - 2 * bit * lax.rem(lax.div(v, bit), 2)


def greet(targets):
    barrier = pltpu.get_barrier_semaphore()
    for t in targets:
        pl.semaphore_signal(barrier, inc=1, device_id=t, device_id_type=MESH)
    pl.semaphore_wait(barrier, len(targets))


def join_rows(parts, width, total):
    have = parts[0].shape[1]
    acc = None
    for k, v in enumerate(parts):
        if have < total:
            v = jnp.concatenate([v, jnp.zeros((v.shape[0], total - have), v.dtype)], axis=1)
        elif have > total:
            v = v[:, :total]
        v = v if k == 0 else pltpu.roll(v, k * width, 1)
        acc = v if acc is None else acc + v
    return acc


def gather_kernel(
    dims, win_ref, wout_ref, small_ref, in_ref, out_ref, par_ref, head_ref,
    small_all, send_sem, recv_sem, local_sem,
):
    cw, gw, nw, hw = dims
    rep, s = peers()
    core, z = lax.rem(rep, 2), lax.div(rep, 2)
    par = lax.rem(z, 2)
    x_s, y_s, d_s = flip(s, 1), flip(s, 2), flip(flip(s, 1), 2)
    core_r, z_r = flip(rep, 1), flip(rep, 2)
    greet([(rep, x_s), (rep, y_s), (rep, d_s), (core_r, s), (z_r, s)])
    made = []

    def send(src, dst, to):
        k = len(made)
        c = pltpu.make_async_remote_copy(
            src_ref=src, dst_ref=dst, send_sem=send_sem.at[k], recv_sem=recv_sem.at[k],
            device_id=to, device_id_type=MESH,
        )
        c.start()
        made.append(c)
        return c

    smalls = [send(small_ref, small_all.at[s], (rep, to)) for to in (x_s, y_s, d_s)]
    small_own = pltpu.make_async_copy(small_ref, small_all.at[s], local_sem.at[2])
    small_own.start()
    locals_ = [small_own]
    arrays = [(win_ref, in_ref), (wout_ref, out_ref)]

    def rows(a, c, q, h):
        half = arrays[a][0].shape[0] // 2
        sixth = half // 6
        return pl.ds(pl.multiple_of(c * half + q * (2 * sixth) + h * sixth, sixth), sixth)

    own, other = 2 * par, 2 - 2 * par
    first = {}
    for q in (own, 1):
        qk = "s" if isinstance(q, int) else "o"
        for a in (1, 0):
            src, dst = arrays[a]
            for h in (0, 1):
                r = rows(a, core, q, h)
                order = ((x_s, "x"), (y_s, "y")) if h == 0 else ((y_s, "y"), (x_s, "x"))
                for to, name in order:
                    first[qk, a, h, name] = send(src.at[r], dst.at[s, r], (rep, to))
    for a in (0, 1):
        src, dst = arrays[a]
        c = pltpu.make_async_copy(src, dst.at[s], local_sem.at[a])
        c.start()
        locals_.append(c)

    relay, over_z, over_core = {}, [], []

    def spread(a, sh, q, h, up):
        dst = arrays[a][1]
        r = rows(a, core, q, h)
        if up:
            over_z.append((a, sh, h, send(dst.at[sh, r], dst.at[sh, r], (z_r, s))))
        over_core.append(send(dst.at[sh, r], dst.at[sh, r], (core_r, s)))

    for q in (own, 1):
        qk = "s" if isinstance(q, int) else "o"
        for a in (1, 0):
            dst = arrays[a][1]
            for h in (0, 1):
                r = rows(a, core, q, h)
                order = ((x_s, "x"), (y_s, "y")) if h == 0 else ((y_s, "y"), (x_s, "x"))
                for sh, name in order:
                    first[qk, a, h, name].wait_recv()
                    if (name == "x") == (h == 0):
                        to = y_s if h == 0 else x_s
                        relay[qk, a, h] = send(dst.at[sh, r], dst.at[sh, r], (rep, to))
                    spread(a, sh, q, h, qk == "o")
        if qk == "o":
            for c in smalls:
                c.wait_recv()
            small_own.wait()
            n = small_all.shape[0]
            total = par_ref.shape[1]
            taken = lambda lo, hi: [small_all[k, lo:hi, :] for k in range(n)]
            par_ref[0:5, :] = join_rows(taken(0, 5), cw, total)
            par_ref[5:6, :] = join_rows(taken(5, 6), gw, total)
            par_ref[6:7, :] = join_rows(taken(6, 7), nw, total)
            heads = [
                join_rows([small_all[k, 7:8, j * LANES : (j + 1) * LANES] for k in range(n)], hw, LANES)
                for j in range(3)
            ]
            head_ref[...] = jnp.concatenate(heads + [jnp.zeros((5, LANES), F32)], axis=0)
            lane_head = lax.broadcasted_iota(jnp.int32, (LANES, total), 1) // (gw // hw)
            pick_m = jnp.where(lax.broadcasted_iota(jnp.int32, (LANES, total), 0) == lane_head, 1.0, 0.0)
            wide = lax.dot_general(
                jnp.broadcast_to(heads[2], (8, LANES)), pick_m, (((1,), (0,)), ((), ())),
                preferred_element_type=F32, precision=HIGH,
            )
            par_ref[7:8, :] = wide[0:1, :]
    for q in (own, 1):
        qk = "s" if isinstance(q, int) else "o"
        for a in (1, 0):
            for h in (0, 1):
                relay[qk, a, h].wait_recv()
                spread(a, d_s, q, h, qk == "o")
    for a, sh, h, c in list(over_z):
        c.wait_recv()
        spread(a, sh, other, h, False)
    for c in over_core:
        c.wait_recv()
    for c in locals_[1:]:
        c.wait()
    for c in made:
        c.wait_send()


def gather_call(w_in, w_out, small, n, dims):
    cw, gw, nw, hw = dims
    sds = jax.ShapeDtypeStruct
    vm, anyw = pl.BlockSpec(memory_space=pltpu.VMEM), pl.BlockSpec(memory_space=pl.ANY)
    copies = 96
    full_in, full_out, par, head = pl.pallas_call(
        functools.partial(gather_kernel, dims),
        in_specs=[vm, vm, vm],
        out_specs=[anyw, anyw, vm, vm],
        out_shape=[
            sds((n, *w_in.shape), BF), sds((n, *w_out.shape), BF),
            sds((8, -(-cw * n // LANES) * LANES), F32), sds((8, LANES), F32),
        ],
        scratch_shapes=[
            pltpu.VMEM((n, *small.shape), F32),
            pltpu.SemaphoreType.DMA((copies,)),
            pltpu.SemaphoreType.DMA((copies,)),
            pltpu.SemaphoreType.DMA((3,)),
        ],
        compiler_params=pltpu.CompilerParams(
            collective_id=0, has_side_effects=True, vmem_limit_bytes=40 * 1024 * 1024
        ),
    )(w_in, w_out, small)
    return full_in.reshape(-1, w_in.shape[1]), full_out.reshape(-1, w_out.shape[1]), par, head


def reduce_kernel(
    dims, lead, gin_ref, gout_ref, dpar_ref, dhead_ref, fin_ref, fout_ref, fs_ref,
    pin, pout, psm, bin1, bout1, bsm1, bin2, bout2, bsm2, cin, cout, csm, tin, tout,
    send_sem, recv_sem,
):
    cw, gw, nw, hw = dims
    rep, s = peers()
    core, z = lax.rem(rep, 2), lax.div(rep, 2)
    mid = (z == 1) | (z == 2)
    x_s, y_s, d_s = flip(s, 1), flip(s, 2), flip(flip(s, 1), 2)
    core_r, pair_r, mid_r = flip(rep, 1), flip(rep, 2), (3 - z) * 2 + core
    n = psm.shape[0]
    count = [0]

    def remote(src, dst, to):
        k = count[0]
        count[0] += 1
        return pltpu.make_async_remote_copy(
            src_ref=src, dst_ref=dst, send_sem=send_sem.at[k], recv_sem=recv_sem.at[k],
            device_id=to, device_id_type=MESH,
        )

    big = [
        (gin_ref, fin_ref, pin, bin1, bin2, cin, tin),
        (gout_ref, fout_ref, pout, bout1, bout2, cout, tout),
    ]

    def piece(a, k, rows, alpha):
        g, fin, p, b1, b2, c, t = big[a]
        half = p.shape[1]
        r = pl.ds(k * rows, rows)
        mine = pl.ds(pl.multiple_of(core * half + k * rows, rows), rows)
        theirs = pl.ds(pl.multiple_of((1 - core) * half + k * rows, rows), rows)
        one, two = (x_s, y_s) if alpha else (y_s, x_s)
        up = lambda v: v.astype(F32)
        st = {}

        def s0():
            st["a"] = remote(g.at[:, theirs], p.at[:, r], (core_r, s))
            st["a"].start()

        def s1():
            st["a"].wait_recv()
            for sh in (one, d_s):
                p[sh, r] = (up(p[sh, r]) + up(g[sh, mine])).astype(BF)
            st["b0"] = remote(p.at[d_s, r], b1.at[1, r], (rep, one))
            st["b0"].start()
            st["b1"] = remote(p.at[one, r], b1.at[0, r], (rep, one))
            st["b1"].start()

        def s2():
            st["b0"].wait_recv()
            p[two, r] = (up(p[two, r]) + up(g[two, mine]) + up(b1[1, r])).astype(BF)
            st["c"] = remote(p.at[two, r], b2.at[r], (rep, two))
            st["c"].start()

        def s3():
            st["b1"].wait_recv()
            st["c"].wait_recv()
            total = up(p[s, r]) + up(g[s, mine]) + up(b1[0, r]) + up(b2[r])
            p[s, r] = total.astype(BF)
            st["z1"] = remote(p.at[s, r], c.at[0, r], (pair_r, s))

            @pl.when(jnp.logical_not(mid))
            def _():
                st["z1"].start()

        def s4():
            st["z2"] = remote(t.at[r], c.at[1, r], (mid_r, s))

            @pl.when(mid)
            def _():
                st["z1"].wait_recv()
                t[r] = (up(p[s, r]) + up(c[0, r])).astype(BF)
                st["z2"].start()

        def s5():
            st["z3"] = remote(fin.at[core, r], fin.at[core, r], (pair_r, s))
            st["f"] = remote(fin.at[core, r], fin.at[core, r], (core_r, s))

            @pl.when(mid)
            def _():
                st["z2"].wait_recv()
                fin[core, r] = (up(t[r]) + up(c[1, r])).astype(BF)
                st["z3"].start()
                st["f"].start()

        def s6():
            @pl.when(jnp.logical_not(mid))
            def _():
                st["z3"].wait_recv()
                st["f"].start()

        def s7():
            st["f"].wait_recv()
            st["f"].wait_send()
            for name in ("a", "b0", "b1", "c"):
                st[name].wait_send()

            @pl.when(mid)
            def _():
                st["z2"].wait_send()
                st["z3"].wait_send()

            @pl.when(jnp.logical_not(mid))
            def _():
                st["z1"].wait_send()

        return [s0, s1, s2, s3, s4, s5, s6, s7]

    def small_piece():
        st = {}

        def s0():
            dpar, dh = dpar_ref[...], dhead_ref[...]
            wide = fs_ref.shape[1]
            back = lambda v, k: (v if k == 0 else pltpu.roll(v, v.shape[1] - k, 1))
            for k in range(n):
                head = back(dh, k * hw)
                row = jnp.concatenate([head[j : j + 1, :] for j in range(3)], axis=1)
                if wide > 3 * LANES:
                    row = jnp.concatenate([row, jnp.zeros((1, wide - 3 * LANES), F32)], axis=1)
                csm[2 + k] = jnp.concatenate(
                    [
                        back(dpar, k * cw)[0:5, :wide], back(dpar, k * gw)[5:6, :wide],
                        back(dpar, k * nw)[6:7, :wide], row,
                    ],
                    axis=0,
                )
            st["a"] = remote(csm.at[pl.ds(2, n)], psm, (core_r, s))
            st["a"].start()

        def s1():
            st["a"].wait_recv()
            for k in range(n):
                psm[k] = psm[k] + csm[2 + k]
            st["b0"] = remote(psm.at[d_s], bsm1.at[1], (rep, x_s))
            st["b0"].start()
            st["b1"] = remote(psm.at[x_s], bsm1.at[0], (rep, x_s))
            st["b1"].start()

        def s2():
            st["b0"].wait_recv()
            psm[y_s] = psm[y_s] + bsm1[1]
            st["c"] = remote(psm.at[y_s], bsm2, (rep, y_s))
            st["c"].start()

        def s3():
            st["b1"].wait_recv()
            st["c"].wait_recv()
            psm[s] = psm[s] + bsm1[0] + bsm2[...]
            st["z1"] = remote(psm.at[s], csm.at[0], (pair_r, s))

            @pl.when(jnp.logical_not(mid))
            def _():
                st["z1"].start()

        def s4():
            st["z2"] = remote(bsm1.at[2], csm.at[1], (mid_r, s))

            @pl.when(mid)
            def _():
                st["z1"].wait_recv()
                bsm1[2] = psm[s] + csm[0]
                st["z2"].start()

        def s5():
            st["z3"] = remote(fs_ref, fs_ref, (pair_r, s))

            @pl.when(mid)
            def _():
                st["z2"].wait_recv()
                fs_ref[...] = bsm1[2] + csm[1]
                st["z3"].start()

        def s6():
            @pl.when(jnp.logical_not(mid))
            def _():
                st["z3"].wait_recv()

        def s7():
            for name in ("a", "b0", "b1", "c"):
                st[name].wait_send()

            @pl.when(mid)
            def _():
                st["z2"].wait_send()
                st["z3"].wait_send()

            @pl.when(jnp.logical_not(mid))
            def _():
                st["z1"].wait_send()

        return [s0, s1, s2, s3, s4, s5, s6, s7]

    pieces = []
    for a in (1, 0):
        half = big[a][2].shape[1]
        for k in range(6):
            pieces.append(piece(a, k, half // 6, k % 2 == 0))
    pieces.insert(1, small_piece())
    greet([(core_r, s), (rep, x_s), (rep, y_s), (pair_r, s), (mid_r, s)])
    for p in pieces:
        p[0]()
    total = len(pieces)
    for t in range(total + lead[-1]):
        for stage, lag in enumerate(lead):
            k = t - lag
            if 0 <= k < total:
                pieces[k][stage + 1]()
    for p in pieces:
        p[7]()


def reduce_call(g_in, g_out, dpar, dhead, n, dims):
    cw, gw, nw, hw = dims
    wide = -(-max(cw, 3 * LANES) // LANES) * LANES
    h_in, w_in = g_in.shape[0] // n // 2, g_in.shape[1]
    h_out, w_out = g_out.shape[0] // n // 2, g_out.shape[1]
    sds = jax.ShapeDtypeStruct
    vm = pl.BlockSpec(memory_space=pltpu.VMEM)
    both = lambda lead: [pltpu.VMEM((*lead, h_in, w_in), BF), pltpu.VMEM((*lead, h_out, w_out), BF)]
    sm = lambda k: pltpu.VMEM((k, 8, wide), F32)
    copies = 13 * 10
    fin, fout, fs = pl.pallas_call(
        functools.partial(reduce_kernel, dims, (0, 2, 4, 5, 6, 7)),
        in_specs=[vm] * 4,
        out_specs=[vm] * 3,
        out_shape=[sds((2, h_in, w_in), BF), sds((2, h_out, w_out), BF), sds((8, wide), F32)],
        scratch_shapes=[
            *both((n,)), sm(n), *both((2,)), sm(3), *both(()), pltpu.VMEM((8, wide), F32),
            *both((2,)), sm(2 + n), *both(()),
            pltpu.SemaphoreType.DMA((copies,)), pltpu.SemaphoreType.DMA((copies,)),
        ],
        compiler_params=pltpu.CompilerParams(
            collective_id=1, has_side_effects=True, vmem_limit_bytes=56 * 1024 * 1024
        ),
    )(g_in.reshape(n, 2 * h_in, w_in), g_out.reshape(n, 2 * h_out, w_out), dpar, dhead)
    return fin.reshape(-1, w_in).astype(F32), fout.reshape(-1, w_out).astype(F32), fs


def pack_small(shards, wide):
    taps, bias, step, decay, skip, norm, gate = [p.astype(F32) for p in shards]
    taps_n = taps.shape[0]
    put = lambda v, row, lane: jnp.pad(
        v, ((row, 8 - row - v.shape[0]), (lane, wide - lane - v.shape[1]))
    )
    return (
        put(taps, 0, 0) + put(bias[None], taps_n, 0) + put(gate[None], 5, 0) + put(norm[None], 6, 0)
        + put(step[None], 7, 0) + put(decay[None], 7, LANES) + put(skip[None], 7, 2 * LANES)
    )


def on_device(tokens, cotangent, doc_lengths, *shards):
    n, chips = lax.axis_size("shard"), lax.axis_size("replica") // 2
    me, rep = lax.axis_index("shard"), lax.axis_index("replica")
    core, chip = lax.rem(rep, 2), lax.div(rep, 2)
    cw, gw, nw, hw = shards[2].shape[1], shards[8].shape[0], shards[7].shape[0], shards[4].shape[0]
    dims = (cw, gw, nw, hw)
    wide = -(-max(cw, gw, nw, 3 * LANES) // LANES) * LANES
    small = pack_small(shards[2:], wide)
    direct = n == 4 and chips == 4
    if direct:
        in_full, out_full, par, head = gather_call(shards[0], shards[1], small, n, dims)
    else:
        small_all = ring_all(small, me, n, shard_step)
        out_full = gather_weight(shards[1], core, me, n)
        in_full = gather_weight(shards[0], core, me, n)
        total = n * cw
        row = lambda r0, r1, w, at: jnp.pad(
            small_all[:, r0:r1, at : at + w].transpose(1, 0, 2).reshape(r1 - r0, n * w),
            ((0, 0), (0, total - n * w)),
        )
        heads = [row(7, 8, hw, k * LANES) for k in range(3)]
        skip_row = jnp.pad(jnp.repeat(heads[2][:, : n * hw], gw // hw, axis=1), ((0, 0), (0, total - n * gw)))
        par = jnp.concatenate([row(0, 5, cw, 0), row(5, 6, gw, 0), row(6, 7, nw, 0), skip_row])
        head = jnp.pad(jnp.concatenate([h[:, :LANES] for h in heads]), ((0, 5), (0, 0)))
    layer, input_grad, grad_in, grad_out, dpar, dhead = device_part(
        tokens, cotangent, doc_lengths[0], in_full, out_full, par, head, n, dims
    )
    if direct:
        big_in, big_out, mine = reduce_call(grad_in.astype(BF), grad_out.astype(BF), dpar, dhead, n, dims)
    else:
        blocks = []
        for k in range(n):
            fit = lambda v, w: jnp.pad(v[:, k * w : (k + 1) * w], ((0, 0), (0, wide - w)))
            last = [jnp.pad(dhead[j : j + 1, k * hw : (k + 1) * hw], ((0, 0), (0, LANES - hw))) for j in range(3)]
            last = jnp.concatenate(last, axis=1)
            blocks.append(jnp.concatenate([
                fit(dpar[:5], cw), fit(dpar[5:6], gw), fit(dpar[6:7], nw),
                jnp.pad(last, ((0, 0), (0, wide - 3 * LANES))),
            ]).reshape(-1, LANES))
        unit = 2 * chips * 8
        packed = jnp.stack(blocks)
        size = packed.shape[1]
        packed = jnp.pad(packed, ((0, 0), (0, -size % unit), (0, 0))).reshape(-1, LANES)
        reduce = functools.partial(reduce_grad, core=core, me=me, n=n, chip=chip, chips=chips)
        big_out = reduce(grad_out, kind=BF)
        big_in = reduce(grad_in, kind=BF)
        mine = reduce(packed, kind=F32)[:size].reshape(8, wide)
    outs = [
        mine[0:4, :cw], mine[4, :cw], mine[7, :hw], mine[7, LANES : LANES + hw],
        mine[7, 2 * LANES : 2 * LANES + hw], mine[6, :nw], mine[5, :gw],
    ]
    return (layer, input_grad, big_in, big_out, *outs)


def solution(mesh):
    tok = P(("replica", "shard"), None)
    weights = (P("shard", None), P("shard", None), P(None, "shard")) + (P("shard"),) * 6
    return jax.shard_map(
        on_device,
        mesh=mesh,
        in_specs=(tok, tok, tok) + weights,
        out_specs=(tok, tok) + weights,
        check_vma=False,
    )
```

```python
import functools

import jax
import jax.numpy as jnp
from jax import lax
from jax.experimental import pallas as pl
from jax.experimental.pallas import tpu as pltpu
from jax.sharding import PartitionSpec as P

BLOCK = 256
LANES = 128
EPS = 1e-05
HIGH = lax.Precision.HIGHEST
BF = jnp.bfloat16
F32 = jnp.float32


def dot(a, b, dims=((1,), (0,)), precision=None):
    return lax.dot_general(a, b, (dims, ((), ())), preferred_element_type=F32, precision=precision)


def prenorm(values, gain_vec):
    scales = lax.rsqrt(jnp.mean(values * values, axis=1, keepdims=True) + EPS)
    return values * scales * gain_vec[None, :]


def segments_of(lengths, length):
    boundary = jnp.cumsum(lengths)
    places = jnp.arange(length, dtype=jnp.int32)
    segment = jnp.sum((places[:, None] >= boundary[None, :]).astype(jnp.int32), axis=1)
    return (segment, places < boundary[-1])


def conv_causal(values, masks, kernel_taps, bias_row):
    kernel_len = kernel_taps.shape[0]
    result = bias_row[None, :] + kernel_taps[kernel_len - 1][None, :] * values
    for offset in range(1, kernel_len):
        shifted = jnp.concatenate(
            [jnp.zeros((offset, values.shape[1]), values.dtype), values[:-offset]], axis=0
        )
        result = result + kernel_taps[kernel_len - 1 - offset][None, :] * jnp.where(
            masks[offset - 1][:, None], shifted, 0.0
        )
    return result


def mixer_kernel(
    inner, taps_n, block, width,
    z_ref, cin_ref, gm_ref, par_ref, mask_ref, gram_ref, gramb_ref, gramt_ref,
    rows_ref, cols_ref, fac_ref,
    dz_ref, dcin_ref, mixed_ref, dgram_ref, dc_ref, ddt_ref, sums_ref,
    pre_s, sp_s, sz_s, ub_s, yd_s, yo_s, mix_s, ss_s, q_s, pad_s, dpad_s,
):
    phase, g = pl.program_id(0), pl.program_id(1)
    taps_ref = par_ref.at[0:4]
    bias_ref, gain_ref, skip_ref = par_ref.at[4:5], par_ref.at[5:6], par_ref.at[7:8]
    length = z_ref.shape[0]
    nb = length // block
    heads = LANES // width
    half = block // 2

    def col(k, rows):
        parts = [
            jnp.broadcast_to(cols_ref[0, rows, k * heads + h : k * heads + h + 1], (block, width))
            for h in range(heads)
        ]
        return jnp.concatenate(parts, axis=1)

    blocks = [slice(i * block, (i + 1) * block) for i in range(nb)]
    up = lambda v: v.astype(F32)

    def decay_of(h, r0, r1, c0, c1):
        spread = cols_ref[0, r0:r1, h : h + 1] - rows_ref[0, h : h + 1, c0:c1]
        return jnp.exp(jnp.minimum(spread, 0.0))

    @pl.when((phase == 0) & (g == 0))
    def _():
        ss_s[...] = jnp.zeros_like(ss_s)
        q_s[...] = jnp.zeros_like(q_s)
        dgram_ref[...] = jnp.zeros_like(dgram_ref)
        dc_ref[...] = jnp.zeros_like(dc_ref)
        ddt_ref[...] = jnp.zeros_like(ddt_ref)
        pad_s[0:8, :] = jnp.zeros((8, LANES), F32)
        dpad_s[length : length + 8, :] = jnp.zeros((8, LANES), F32)

    pad_s[8 : 8 + length, :] = cin_ref[...]

    @pl.when(phase == 0)
    def _():
        vs = []
        for i in range(nb):
            r = blocks[i]
            r0, rm, r1 = i * block, i * block + half, (i + 1) * block
            p_r = bias_ref[0:1, :] + taps_ref[taps_n - 1 : taps_n, :] * cin_ref[r, :]
            for k in range(1, taps_n):
                p_r = p_r + taps_ref[taps_n - 1 - k : taps_n - k, :] * (
                    pad_s[8 - k + r0 : 8 - k + r1, :] * mask_ref[k - 1, r0:r1, :]
                )
            pre_s[g, r, :] = p_r
            sp = jax.nn.sigmoid(p_r)
            sp_s[g, r, :] = sp
            x = p_r * sp
            u = x * col(1, r)
            ub = u.astype(BF)
            ub_s[g, r, :] = ub
            vs.append((up(ub) * col(3, r)).astype(BF))
            tops, bots = [], []
            for h in range(heads):
                lanes = slice(h * width, (h + 1) * width)
                top = (decay_of(h, r0, rm, r0, rm) * gram_ref[r0:rm, r0:rm]).astype(BF)
                bot = (decay_of(h, rm, r1, r0, r1) * gram_ref[rm:r1, r0:r1]).astype(BF)
                mix_s[g, h, i, 0:half, 0:half] = top
                mix_s[g, h, i, half:block, :] = bot
                tops.append(dot(top, ub[0:half, lanes]))
                bots.append(dot(bot, ub[:, lanes]))
            yd = jnp.concatenate([jnp.concatenate(tops, axis=1), jnp.concatenate(bots, axis=1)], axis=0)
            yd_s[g, r, :] = yd
            y = yd + skip_ref[0:1, :] * x
            if i:
                yo = jnp.zeros((block, LANES), F32)
                for j in range(i):
                    yo = yo + dot(gramb_ref[r, blocks[j]], vs[j]) * fac_ref[i * nb + j : i * nb + j + 1, :]
                yo_s[g, r, :] = yo
                y = y + yo * col(2, r)
            z = z_ref[r, :]
            sz = jax.nn.sigmoid(z)
            sz_s[g, r, :] = sz
            gated = y * (z * sz)
            ss_s[r, :] += gated * gated
            q_s[r, :] += gm_ref[r, :] * gain_ref[0:1, :] * gated

    @pl.when((phase == 1) & (g == 0))
    def _():
        scale = lax.rsqrt(jnp.sum(ss_s[...], axis=1, keepdims=True) / inner + EPS)
        coef = jnp.sum(q_s[...], axis=1, keepdims=True) * scale * scale * scale / inner
        ss_s[...] = jnp.broadcast_to(scale, ss_s.shape)
        q_s[...] = jnp.broadcast_to(coef, q_s.shape)

    @pl.when(phase == 1)
    def _():
        lane = lax.broadcasted_iota(jnp.int32, (LANES, LANES), 0) // width
        target = lax.broadcasted_iota(jnp.int32, (LANES, LANES), 1)
        pick = jnp.where(lane + g * heads == target, 1.0, 0.0).astype(BF)

        def by_head(d):
            hi = d.astype(BF)
            lo = (d - hi.astype(F32)).astype(BF)
            return dot(hi, pick) + dot(lo, pick)

        ws = []
        dskip = jnp.zeros((1, LANES), F32)
        dgain = jnp.zeros((1, LANES), F32)
        for i in range(nb):
            r = blocks[i]
            x = pre_s[g, r, :] * sp_s[g, r, :]
            z = z_ref[r, :]
            sig = sz_s[g, r, :]
            act = z * sig
            y = yd_s[g, r, :] + skip_ref[0:1, :] * x
            if i:
                a = col(2, r)
                y = y + yo_s[g, r, :] * a
            gated = y * act
            normal = gated * ss_s[r, :]
            mixed_ref[r, :] = (normal * gain_ref[0:1, :]).astype(BF)
            gm = gm_ref[r, :]
            dgain = dgain + jnp.sum(gm * normal, axis=0, keepdims=True)
            dgated = gm * gain_ref[0:1, :] * ss_s[r, :] - gated * q_s[r, :]
            dz_ref[r, :] = (dgated * y * (sig + act * (1.0 - sig))).astype(BF)
            dy = dgated * act
            dskip = dskip + jnp.sum(dy * x, axis=0, keepdims=True)
            dpad_s[r, :] = dy
            ws.append((dy * a).astype(BF) if i else None)
        for j in range(nb):
            r = blocks[j]
            r0, rm, r1 = j * block, j * block + half, (j + 1) * block
            dy = dpad_s[r, :]
            dyb = dy.astype(BF)
            dyt = jnp.transpose(dy).astype(BF)
            ub = ub_s[g, r, :]
            dut = []
            tops, bots = jnp.zeros((half, half), F32), jnp.zeros((half, block), F32)
            for h in range(heads):
                lanes = slice(h * width, (h + 1) * width)
                left = dot(dyt[lanes, :], mix_s[g, h, j, :, 0:half])
                right = dot(dyt[lanes, half:block], mix_s[g, h, j, half:block, half:block])
                dut.append(jnp.concatenate([left, right], axis=1))
                tops = tops + decay_of(h, r0, rm, r0, rm) * dot(
                    dyb[0:half, lanes], ub[0:half, lanes], ((1,), (1,))
                )
                bots = bots + decay_of(h, rm, r1, r0, r1) * dot(
                    dyb[half:block, lanes], ub[:, lanes], ((1,), (1,))
                )
            dgram_ref[r0:rm, r0:rm] += tops
            dgram_ref[rm:r1, r0:r1] += bots
            du = jnp.transpose(jnp.concatenate(dut, axis=0))
            uf = up(ub)
            dcum = up(dyb) * yd_s[g, r, :] - uf * du
            if j:
                dcum = dcum + up(ws[j]) * yo_s[g, r, :]
            if j < nb - 1:
                leave = col(3, r)
                v = (uf * leave).astype(BF)
                dv = jnp.zeros((block, LANES), F32)
                for i in range(j + 1, nb):
                    fac = fac_ref[i * nb + j : i * nb + j + 1, :]
                    dv = dv + dot(gramt_ref[r, blocks[i]], ws[i]) * fac
                    dgram_ref[blocks[i], r] += dot((up(ws[i]) * fac).astype(BF), v, ((1,), (1,)))
                dcum = dcum - up(v) * dv
                du = du + dv * leave
            dc_ref[r, :] += by_head(dcum)
            sig = sp_s[g, r, :]
            x = pre_s[g, r, :] * sig
            ddt_ref[r, :] += by_head(du * x)
            dx = skip_ref[0:1, :] * dy + du * col(1, r)
            dpad_s[r, :] = dx * (sig + x * (1.0 - sig))
        acc = [jnp.zeros((1, LANES), F32) for _ in range(taps_n + 1)]
        total = lambda v: jnp.sum(v, axis=0, keepdims=True)
        for i in range(nb):
            r0, r1 = i * block, (i + 1) * block
            dpre = dpad_s[r0:r1, :]
            dcin = taps_ref[taps_n - 1 : taps_n, :] * dpre
            acc[taps_n - 1] = acc[taps_n - 1] + total(dpre * cin_ref[r0:r1, :])
            acc[taps_n] = acc[taps_n] + total(dpre)
            for k in range(1, taps_n):
                dcin = dcin + taps_ref[taps_n - 1 - k : taps_n - k, :] * (
                    dpad_s[r0 + k : r1 + k, :] * mask_ref[k - 1, r0 + k : r1 + k, :]
                )
                acc[taps_n - 1 - k] = acc[taps_n - 1 - k] + total(
                    dpre * mask_ref[k - 1, r0:r1, :] * pad_s[8 - k + r0 : 8 - k + r1, :]
                )
            dcin_ref[r0:r1, :] = dcin.astype(BF)
        sums_ref[...] = jnp.concatenate(acc + [dgain, dskip, jnp.zeros((1, LANES), F32)], axis=0)


def mixer_call(projected, gm, par, inner, taps_n, conv_masks, gram, spacing, cum, heads_all):
    length = projected.shape[0]
    width = inner // heads_all
    heads = LANES // width
    groups = inner // LANES
    block = BLOCK
    nb = length // block
    ends = cum[block - 1 :: block]
    starts = jnp.concatenate([jnp.zeros((1, heads_all), F32), ends[:-1]], axis=0)
    cum_b = cum.reshape(nb, block, heads_all)
    enter = jnp.exp(cum_b - starts[:, None]).reshape(length, heads_all)
    leave = jnp.exp(ends[:, None] - cum_b).reshape(length, heads_all)
    fac = jnp.exp(jnp.minimum(starts[:, None] - ends[None, :], 0.0)).reshape(nb * nb, heads_all)
    fac = jnp.repeat(fac, width, axis=1)
    cols = jnp.stack([cum, spacing, enter, leave], axis=1).reshape(length, 4, groups, heads)
    cols = cols.transpose(2, 0, 1, 3).reshape(groups, length, 4 * heads)
    rows = cum.T.reshape(groups, heads, length)
    wide = lambda m: jnp.broadcast_to(m[:, None], (length, LANES)).astype(F32)
    masks = jnp.pad(jnp.stack([wide(m) for m in conv_masks]), ((0, 0), (0, 8), (0, 0)))
    gram_b = gram.astype(BF)
    n_sum = 8

    part = lambda off: pl.BlockSpec((length, LANES), lambda p, g: (0, off + g))
    row = lambda n: pl.BlockSpec((n, LANES), lambda p, g: (0, g))
    full = lambda *s: pl.BlockSpec(s, lambda p, g: (0,) * len(s))
    late = lambda n: pl.BlockSpec((n, LANES), lambda p, g: (0, p * g))
    sds = jax.ShapeDtypeStruct
    return pl.pallas_call(
        functools.partial(mixer_kernel, inner, taps_n, block, width),
        grid=(2, groups),
        in_specs=[
            part(0), part(groups), part(0), row(8),
            full(taps_n - 1, length + 8, LANES), full(length, length),
            full(length, length), full(length, length),
            pl.BlockSpec((1, heads, length), lambda p, g: (g, 0, 0)),
            pl.BlockSpec((1, length, 4 * heads), lambda p, g: (g, 0, 0)),
            row(nb * nb),
        ],
        out_specs=[
            late(length), late(length), late(length), full(length, length),
            full(length, LANES), full(length, LANES), late(n_sum),
        ],
        out_shape=[
            sds((length, inner), BF), sds((length, inner), BF), sds((length, inner), BF),
            sds((length, length), F32), sds((length, LANES), F32), sds((length, LANES), F32),
            sds((n_sum, inner), F32),
        ],
        scratch_shapes=[
            pltpu.VMEM((groups, length, LANES), F32),
            pltpu.VMEM((groups, length, LANES), F32),
            pltpu.VMEM((groups, length, LANES), F32),
            pltpu.VMEM((groups, length, LANES), BF),
            pltpu.VMEM((groups, length, LANES), F32),
            pltpu.VMEM((groups, length, LANES), F32),
            pltpu.VMEM((groups, heads, nb, block, block), BF),
            pltpu.VMEM((length, LANES), F32),
            pltpu.VMEM((length, LANES), F32),
            pltpu.VMEM((length + 8, LANES), F32),
            pltpu.VMEM((length + 8, LANES), F32),
        ],
        compiler_params=pltpu.CompilerParams(
            vmem_limit_bytes=60 * 1024 * 1024, dimension_semantics=("arbitrary", "arbitrary")
        ),
        cost_estimate=pl.CostEstimate(
            flops=20 * length * block * inner, bytes_accessed=40 * length * inner, transcendentals=0
        ),
    )(
        projected, projected, gm, par, masks, gram, gram_b, gram_b.T, rows, cols, fac,
    )


def device_part(tokens, cotangent, lengths, in_full, out_full, par, head, n, dims):
    cw, gw, nw, hw = dims
    length = tokens.shape[0]
    segment, valid = segments_of(lengths, length)
    inner, channels, heads_all = n * gw, n * cw, n * hw
    taps, bias = par[0:4, :channels], par[4, :channels]
    step_bias, decay_log = head[0, :heads_all], head[1, :heads_all]
    gain_vec = par[6, : n * nw]
    state = (channels - inner) // 2
    values = tokens.astype(F32)
    normed = prenorm(values, gain_vec).astype(BF)
    projected = dot(normed, in_full)
    masked = cotangent * valid.astype(BF)[:, None]
    grad_mixed = dot(masked, out_full, ((1,), (1,)))
    places = jnp.arange(length, dtype=jnp.int32)
    lower = places[:, None] >= places[None, :]
    conv_masks = [
        (places >= k) & (jnp.roll(segment, k) == segment) for k in range(1, taps.shape[0])
    ]
    same = lower & (segment[:, None] == segment[None, :])

    def gram_of(cin, taps_bc, bias_bc):
        out = jax.nn.silu(conv_causal(cin, conv_masks, taps_bc, bias_bc))
        return jnp.where(same, dot(out[:, state:], out[:, :state], ((1,), (1,)), HIGH), 0.0)

    def steps_of(raw, shift, logs):
        spacing = jax.nn.softplus(raw + shift[None, :])
        cum = dot(lower.astype(F32), spacing * -jnp.exp(logs)[None, :], precision=HIGH)
        return spacing, cum

    gram, gram_back = jax.vjp(
        gram_of, projected[:, 2 * inner : inner + channels], taps[:, inner:], bias[inner:]
    )
    (spacing, cum), steps_back = jax.vjp(
        steps_of, projected[:, inner + channels :], step_bias, decay_log
    )
    dz, dcin, mixed, dgram, dcum, dspacing, sums = mixer_call(
        projected, grad_mixed, par, inner, taps.shape[0], conv_masks, gram, spacing, cum, heads_all
    )
    d_bc, dtaps_bc, dbias_bc = gram_back(dgram)
    d_raw, d_shift, d_logs = steps_back((dspacing[:, :heads_all], dcum[:, :heads_all]))
    d_skip = jnp.sum(sums[6].reshape(heads_all, -1), axis=1)
    grad_proj = jnp.concatenate([dz, dcin, d_bc.astype(BF), d_raw.astype(BF)], axis=1)
    layer = values + valid.astype(F32)[:, None] * dot(mixed, out_full)
    grad_outw = dot(mixed, masked, ((0,), (0,)))
    grad_inw = dot(normed, grad_proj, ((0,), (0,)))
    grad_normed = dot(grad_proj, in_full, ((1,), (1,)))
    _, norm_back = jax.vjp(prenorm, values, gain_vec)
    grad_norm_in, grad_gain = norm_back(grad_normed)
    input_grad = cotangent.astype(F32) + grad_norm_in
    fit = lambda v, w: jnp.pad(v, ((0, 0), (0, w - v.shape[1])))
    dpar = jnp.concatenate([
        jnp.concatenate([sums[:5], jnp.concatenate([dtaps_bc, dbias_bc[None]])], axis=1),
        fit(sums[5:6], channels), fit(grad_gain[None], channels), jnp.zeros((1, channels), F32),
    ])
    dhead = jnp.pad(jnp.stack([d_shift, d_logs, d_skip]), ((0, 5), (0, LANES - heads_all)))
    return layer, input_grad, grad_inw, grad_outw, dpar, dhead


def moved(x, step):
    n_rep, n = lax.axis_size("replica"), lax.axis_size("shard")
    perm = []
    for r in range(n_rep):
        for s in range(n):
            to_r, to_s = step(r, s)
            perm.append((r * n + s, to_r * n + to_s))
    return lax.ppermute(x, ("replica", "shard"), perm)


def pick(x, i):
    return lax.dynamic_index_in_dim(x, i, 0, keepdims=False)


def ring_all(x, index, n, step):
    got = jnp.stack([x] + [moved(x, functools.partial(step, k)) for k in range(1, n)])
    return jnp.stack([pick(got, lax.rem(index - j + n, n)) for j in range(n)])


def ring_sum(parts, index, n, step):
    total = pick(parts, index).astype(F32)
    for k in range(1, n):
        total = total + moved(pick(parts, lax.rem(index + k, n)), functools.partial(step, k))
    return total


def shard_step(k, r, s):
    return r, (s + k) % lax.axis_size("shard")


def chip_step(k, r, s):
    return (r + 2 * k) % lax.axis_size("replica"), s


def core_step(r, s):
    return r ^ 1, s


def both_halves(mine, core, axis):
    other = moved(mine, core_step)
    first = jnp.where(core == 0, mine, other)
    second = jnp.where(core == 0, other, mine)
    return jnp.stack([first, second], axis=axis)


def gather_weight(shard, core, me, n):
    half = pick(shard.reshape(2, -1, shard.shape[1]), core)
    mine = ring_all(half, me, n, shard_step)
    return both_halves(mine, core, 1).reshape(-1, shard.shape[1])


def reduce_grad(grad, core, me, n, chip, chips, kind):
    columns = grad.shape[1]
    blocks = grad.astype(kind).reshape(n, 2, -1, columns)
    keep = lax.dynamic_index_in_dim(blocks, core, 1, keepdims=False)
    send = lax.dynamic_index_in_dim(blocks, 1 - core, 1, keepdims=False)
    pair = (keep.astype(F32) + moved(send, core_step).astype(F32)).astype(kind)
    mine = ring_sum(pair, me, n, shard_step).astype(kind)
    piece = ring_sum(mine.reshape(chips, -1, columns), chip, chips, chip_step).astype(kind)
    half = ring_all(piece, chip, chips, chip_step).reshape(-1, columns)
    return both_halves(half, core, 0).reshape(-1, columns).astype(F32)


MESH = pl.DeviceIdType.MESH


def peers():
    rep, s = lax.axis_index("replica"), lax.axis_index("shard")
    return rep, s


def flip(v, bit):
    return v + bit - 2 * bit * lax.rem(lax.div(v, bit), 2)


def greet(targets):
    barrier = pltpu.get_barrier_semaphore()
    for t in targets:
        pl.semaphore_signal(barrier, inc=1, device_id=t, device_id_type=MESH)
    pl.semaphore_wait(barrier, len(targets))


def join_rows(parts, width, total):
    have = parts[0].shape[1]
    acc = None
    for k, v in enumerate(parts):
        if have < total:
            v = jnp.concatenate([v, jnp.zeros((v.shape[0], total - have), v.dtype)], axis=1)
        elif have > total:
            v = v[:, :total]
        v = v if k == 0 else pltpu.roll(v, k * width, 1)
        acc = v if acc is None else acc + v
    return acc


def gather_kernel(
    dims, win_ref, wout_ref, small_ref, in_ref, out_ref, par_ref, head_ref,
    small_all, send_sem, recv_sem, local_sem,
):
    cw, gw, nw, hw = dims
    rep, s = peers()
    core, z = lax.rem(rep, 2), lax.div(rep, 2)
    par = lax.rem(z, 2)
    x_s, y_s, d_s = flip(s, 1), flip(s, 2), flip(flip(s, 1), 2)
    core_r, z_r = flip(rep, 1), flip(rep, 2)
    greet([(rep, x_s), (rep, y_s), (rep, d_s), (core_r, s), (z_r, s)])
    made = []

    def send(src, dst, to):
        k = len(made)
        c = pltpu.make_async_remote_copy(
            src_ref=src, dst_ref=dst, send_sem=send_sem.at[k], recv_sem=recv_sem.at[k],
            device_id=to, device_id_type=MESH,
        )
        c.start()
        made.append(c)
        return c

    smalls = [send(small_ref, small_all.at[s], (rep, to)) for to in (x_s, y_s, d_s)]
    small_own = pltpu.make_async_copy(small_ref, small_all.at[s], local_sem.at[2])
    small_own.start()
    locals_ = [small_own]
    arrays = [(win_ref, in_ref), (wout_ref, out_ref)]

    def rows(a, c, q, h):
        half = arrays[a][0].shape[0] // 2
        sixth = half // 6
        return pl.ds(pl.multiple_of(c * half + q * (2 * sixth) + h * sixth, sixth), sixth)

    own, other = 2 * par, 2 - 2 * par
    first = {}
    for q in (own, 1):
        qk = "s" if isinstance(q, int) else "o"
        for a in (1, 0):
            src, dst = arrays[a]
            for h in (0, 1):
                r = rows(a, core, q, h)
                order = ((x_s, "x"), (y_s, "y")) if h == 0 else ((y_s, "y"), (x_s, "x"))
                for to, name in order:
                    first[qk, a, h, name] = send(src.at[r], dst.at[s, r], (rep, to))
    for a in (0, 1):
        src, dst = arrays[a]
        c = pltpu.make_async_copy(src, dst.at[s], local_sem.at[a])
        c.start()
        locals_.append(c)

    relay, over_z, over_core = {}, [], []

    def spread(a, sh, q, h, up):
        dst = arrays[a][1]
        r = rows(a, core, q, h)
        if up:
            over_z.append((a, sh, h, send(dst.at[sh, r], dst.at[sh, r], (z_r, s))))
        over_core.append(send(dst.at[sh, r], dst.at[sh, r], (core_r, s)))

    for q in (own, 1):
        qk = "s" if isinstance(q, int) else "o"
        for a in (1, 0):
            dst = arrays[a][1]
            for h in (0, 1):
                r = rows(a, core, q, h)
                order = ((x_s, "x"), (y_s, "y")) if h == 0 else ((y_s, "y"), (x_s, "x"))
                for sh, name in order:
                    first[qk, a, h, name].wait_recv()
                    if (name == "x") == (h == 0):
                        to = y_s if h == 0 else x_s
                        relay[qk, a, h] = send(dst.at[sh, r], dst.at[sh, r], (rep, to))
                    spread(a, sh, q, h, qk == "o")
        if qk == "o":
            for c in smalls:
                c.wait_recv()
            small_own.wait()
            n = small_all.shape[0]
            total = par_ref.shape[1]
            taken = lambda lo, hi: [small_all[k, lo:hi, :] for k in range(n)]
            par_ref[0:5, :] = join_rows(taken(0, 5), cw, total)
            par_ref[5:6, :] = join_rows(taken(5, 6), gw, total)
            par_ref[6:7, :] = join_rows(taken(6, 7), nw, total)
            heads = [
                join_rows([small_all[k, 7:8, j * LANES : (j + 1) * LANES] for k in range(n)], hw, LANES)
                for j in range(3)
            ]
            head_ref[...] = jnp.concatenate(heads + [jnp.zeros((5, LANES), F32)], axis=0)
            lane_head = lax.broadcasted_iota(jnp.int32, (LANES, total), 1) // (gw // hw)
            pick_m = jnp.where(lax.broadcasted_iota(jnp.int32, (LANES, total), 0) == lane_head, 1.0, 0.0)
            wide = lax.dot_general(
                jnp.broadcast_to(heads[2], (8, LANES)), pick_m, (((1,), (0,)), ((), ())),
                preferred_element_type=F32, precision=HIGH,
            )
            par_ref[7:8, :] = wide[0:1, :]
    for q in (own, 1):
        qk = "s" if isinstance(q, int) else "o"
        for a in (1, 0):
            for h in (0, 1):
                relay[qk, a, h].wait_recv()
                spread(a, d_s, q, h, qk == "o")
    for a, sh, h, c in list(over_z):
        c.wait_recv()
        spread(a, sh, other, h, False)
    for c in over_core:
        c.wait_recv()
    for c in locals_[1:]:
        c.wait()
    for c in made:
        c.wait_send()


def gather_call(w_in, w_out, small, n, dims):
    cw, gw, nw, hw = dims
    sds = jax.ShapeDtypeStruct
    vm, anyw = pl.BlockSpec(memory_space=pltpu.VMEM), pl.BlockSpec(memory_space=pl.ANY)
    copies = 96
    full_in, full_out, par, head = pl.pallas_call(
        functools.partial(gather_kernel, dims),
        in_specs=[vm, vm, vm],
        out_specs=[anyw, anyw, vm, vm],
        out_shape=[
            sds((n, *w_in.shape), BF), sds((n, *w_out.shape), BF),
            sds((8, -(-cw * n // LANES) * LANES), F32), sds((8, LANES), F32),
        ],
        scratch_shapes=[
            pltpu.VMEM((n, *small.shape), F32),
            pltpu.SemaphoreType.DMA((copies,)),
            pltpu.SemaphoreType.DMA((copies,)),
            pltpu.SemaphoreType.DMA((3,)),
        ],
        compiler_params=pltpu.CompilerParams(
            collective_id=0, has_side_effects=True, vmem_limit_bytes=40 * 1024 * 1024
        ),
    )(w_in, w_out, small)
    return full_in.reshape(-1, w_in.shape[1]), full_out.reshape(-1, w_out.shape[1]), par, head


def reduce_kernel(
    dims, lead, gin_ref, gout_ref, dpar_ref, dhead_ref, fin_ref, fout_ref, fs_ref,
    pin, pout, psm, bin1, bout1, bsm1, bin2, bout2, bsm2, cin, cout, csm, tin, tout,
    send_sem, recv_sem,
):
    cw, gw, nw, hw = dims
    rep, s = peers()
    core, z = lax.rem(rep, 2), lax.div(rep, 2)
    mid = (z == 1) | (z == 2)
    x_s, y_s, d_s = flip(s, 1), flip(s, 2), flip(flip(s, 1), 2)
    core_r, pair_r, mid_r = flip(rep, 1), flip(rep, 2), (3 - z) * 2 + core
    n = psm.shape[0]
    count = [0]

    def remote(src, dst, to):
        k = count[0]
        count[0] += 1
        return pltpu.make_async_remote_copy(
            src_ref=src, dst_ref=dst, send_sem=send_sem.at[k], recv_sem=recv_sem.at[k],
            device_id=to, device_id_type=MESH,
        )

    big = [
        (gin_ref, fin_ref, pin, bin1, bin2, cin, tin),
        (gout_ref, fout_ref, pout, bout1, bout2, cout, tout),
    ]

    def piece(a, k, rows, alpha):
        g, fin, p, b1, b2, c, t = big[a]
        half = p.shape[1]
        r = pl.ds(k * rows, rows)
        mine = pl.ds(pl.multiple_of(core * half + k * rows, rows), rows)
        theirs = pl.ds(pl.multiple_of((1 - core) * half + k * rows, rows), rows)
        one, two = (x_s, y_s) if alpha else (y_s, x_s)
        up = lambda v: v.astype(F32)
        st = {}

        def s0():
            st["a"] = remote(g.at[:, theirs], p.at[:, r], (core_r, s))
            st["a"].start()

        def s1():
            st["a"].wait_recv()
            for sh in (one, d_s):
                p[sh, r] = (up(p[sh, r]) + up(g[sh, mine])).astype(BF)
            st["b0"] = remote(p.at[d_s, r], b1.at[1, r], (rep, one))
            st["b0"].start()
            st["b1"] = remote(p.at[one, r], b1.at[0, r], (rep, one))
            st["b1"].start()

        def s2():
            st["b0"].wait_recv()
            p[two, r] = (up(p[two, r]) + up(g[two, mine]) + up(b1[1, r])).astype(BF)
            st["c"] = remote(p.at[two, r], b2.at[r], (rep, two))
            st["c"].start()

        def s3():
            st["b1"].wait_recv()
            st["c"].wait_recv()
            total = up(p[s, r]) + up(g[s, mine]) + up(b1[0, r]) + up(b2[r])
            p[s, r] = total.astype(BF)
            st["z1"] = remote(p.at[s, r], c.at[0, r], (pair_r, s))

            @pl.when(jnp.logical_not(mid))
            def _():
                st["z1"].start()

        def s4():
            st["z2"] = remote(t.at[r], c.at[1, r], (mid_r, s))

            @pl.when(mid)
            def _():
                st["z1"].wait_recv()
                t[r] = (up(p[s, r]) + up(c[0, r])).astype(BF)
                st["z2"].start()

        def s5():
            st["z3"] = remote(fin.at[core, r], fin.at[core, r], (pair_r, s))
            st["f"] = remote(fin.at[core, r], fin.at[core, r], (core_r, s))

            @pl.when(mid)
            def _():
                st["z2"].wait_recv()
                fin[core, r] = (up(t[r]) + up(c[1, r])).astype(BF)
                st["z3"].start()
                st["f"].start()

        def s6():
            @pl.when(jnp.logical_not(mid))
            def _():
                st["z3"].wait_recv()
                st["f"].start()

        def s7():
            st["f"].wait_recv()
            st["f"].wait_send()
            for name in ("a", "b0", "b1", "c"):
                st[name].wait_send()

            @pl.when(mid)
            def _():
                st["z2"].wait_send()
                st["z3"].wait_send()

            @pl.when(jnp.logical_not(mid))
            def _():
                st["z1"].wait_send()

        return [s0, s1, s2, s3, s4, s5, s6, s7]

    def small_piece():
        st = {}

        def s0():
            dpar, dh = dpar_ref[...], dhead_ref[...]
            wide = fs_ref.shape[1]
            back = lambda v, k: (v if k == 0 else pltpu.roll(v, v.shape[1] - k, 1))
            for k in range(n):
                head = back(dh, k * hw)
                row = jnp.concatenate([head[j : j + 1, :] for j in range(3)], axis=1)
                if wide > 3 * LANES:
                    row = jnp.concatenate([row, jnp.zeros((1, wide - 3 * LANES), F32)], axis=1)
                csm[2 + k] = jnp.concatenate(
                    [
                        back(dpar, k * cw)[0:5, :wide], back(dpar, k * gw)[5:6, :wide],
                        back(dpar, k * nw)[6:7, :wide], row,
                    ],
                    axis=0,
                )
            st["a"] = remote(csm.at[pl.ds(2, n)], psm, (core_r, s))
            st["a"].start()

        def s1():
            st["a"].wait_recv()
            for k in range(n):
                psm[k] = psm[k] + csm[2 + k]
            st["b0"] = remote(psm.at[d_s], bsm1.at[1], (rep, x_s))
            st["b0"].start()
            st["b1"] = remote(psm.at[x_s], bsm1.at[0], (rep, x_s))
            st["b1"].start()

        def s2():
            st["b0"].wait_recv()
            psm[y_s] = psm[y_s] + bsm1[1]
            st["c"] = remote(psm.at[y_s], bsm2, (rep, y_s))
            st["c"].start()

        def s3():
            st["b1"].wait_recv()
            st["c"].wait_recv()
            psm[s] = psm[s] + bsm1[0] + bsm2[...]
            st["z1"] = remote(psm.at[s], csm.at[0], (pair_r, s))

            @pl.when(jnp.logical_not(mid))
            def _():
                st["z1"].start()

        def s4():
            st["z2"] = remote(bsm1.at[2], csm.at[1], (mid_r, s))

            @pl.when(mid)
            def _():
                st["z1"].wait_recv()
                bsm1[2] = psm[s] + csm[0]
                st["z2"].start()

        def s5():
            st["z3"] = remote(fs_ref, fs_ref, (pair_r, s))

            @pl.when(mid)
            def _():
                st["z2"].wait_recv()
                fs_ref[...] = bsm1[2] + csm[1]
                st["z3"].start()

        def s6():
            @pl.when(jnp.logical_not(mid))
            def _():
                st["z3"].wait_recv()

        def s7():
            for name in ("a", "b0", "b1", "c"):
                st[name].wait_send()

            @pl.when(mid)
            def _():
                st["z2"].wait_send()
                st["z3"].wait_send()

            @pl.when(jnp.logical_not(mid))
            def _():
                st["z1"].wait_send()

        return [s0, s1, s2, s3, s4, s5, s6, s7]

    pieces = []
    for a in (1, 0):
        half = big[a][2].shape[1]
        for k in range(6):
            pieces.append(piece(a, k, half // 6, k % 2 == 0))
    pieces.insert(1, small_piece())
    greet([(core_r, s), (rep, x_s), (rep, y_s), (pair_r, s), (mid_r, s)])
    for p in pieces:
        p[0]()
    total = len(pieces)
    for t in range(total + lead[-1]):
        for stage, lag in enumerate(lead):
            k = t - lag
            if 0 <= k < total:
                pieces[k][stage + 1]()
    for p in pieces:
        p[7]()


def reduce_call(g_in, g_out, dpar, dhead, n, dims):
    cw, gw, nw, hw = dims
    wide = -(-max(cw, 3 * LANES) // LANES) * LANES
    h_in, w_in = g_in.shape[0] // n // 2, g_in.shape[1]
    h_out, w_out = g_out.shape[0] // n // 2, g_out.shape[1]
    sds = jax.ShapeDtypeStruct
    vm = pl.BlockSpec(memory_space=pltpu.VMEM)
    both = lambda lead: [pltpu.VMEM((*lead, h_in, w_in), BF), pltpu.VMEM((*lead, h_out, w_out), BF)]
    sm = lambda k: pltpu.VMEM((k, 8, wide), F32)
    copies = 13 * 10
    fin, fout, fs = pl.pallas_call(
        functools.partial(reduce_kernel, dims, (0, 2, 4, 6, 8, 10)),
        in_specs=[vm] * 4,
        out_specs=[vm] * 3,
        out_shape=[sds((2, h_in, w_in), BF), sds((2, h_out, w_out), BF), sds((8, wide), F32)],
        scratch_shapes=[
            *both((n,)), sm(n), *both((2,)), sm(3), *both(()), pltpu.VMEM((8, wide), F32),
            *both((2,)), sm(2 + n), *both(()),
            pltpu.SemaphoreType.DMA((copies,)), pltpu.SemaphoreType.DMA((copies,)),
        ],
        compiler_params=pltpu.CompilerParams(
            collective_id=1, has_side_effects=True, vmem_limit_bytes=56 * 1024 * 1024
        ),
    )(g_in.reshape(n, 2 * h_in, w_in), g_out.reshape(n, 2 * h_out, w_out), dpar, dhead)
    return fin.reshape(-1, w_in).astype(F32), fout.reshape(-1, w_out).astype(F32), fs


def pack_small(shards, wide):
    taps, bias, step, decay, skip, norm, gate = [p.astype(F32) for p in shards]
    taps_n = taps.shape[0]
    put = lambda v, row, lane: jnp.pad(
        v, ((row, 8 - row - v.shape[0]), (lane, wide - lane - v.shape[1]))
    )
    return (
        put(taps, 0, 0) + put(bias[None], taps_n, 0) + put(gate[None], 5, 0) + put(norm[None], 6, 0)
        + put(step[None], 7, 0) + put(decay[None], 7, LANES) + put(skip[None], 7, 2 * LANES)
    )


def on_device(tokens, cotangent, doc_lengths, *shards):
    n, chips = lax.axis_size("shard"), lax.axis_size("replica") // 2
    me, rep = lax.axis_index("shard"), lax.axis_index("replica")
    core, chip = lax.rem(rep, 2), lax.div(rep, 2)
    cw, gw, nw, hw = shards[2].shape[1], shards[8].shape[0], shards[7].shape[0], shards[4].shape[0]
    dims = (cw, gw, nw, hw)
    wide = -(-max(cw, gw, nw, 3 * LANES) // LANES) * LANES
    small = pack_small(shards[2:], wide)
    direct = n == 4 and chips == 4
    if direct:
        in_full, out_full, par, head = gather_call(shards[0], shards[1], small, n, dims)
    else:
        small_all = ring_all(small, me, n, shard_step)
        out_full = gather_weight(shards[1], core, me, n)
        in_full = gather_weight(shards[0], core, me, n)
        total = n * cw
        row = lambda r0, r1, w, at: jnp.pad(
            small_all[:, r0:r1, at : at + w].transpose(1, 0, 2).reshape(r1 - r0, n * w),
            ((0, 0), (0, total - n * w)),
        )
        heads = [row(7, 8, hw, k * LANES) for k in range(3)]
        skip_row = jnp.pad(jnp.repeat(heads[2][:, : n * hw], gw // hw, axis=1), ((0, 0), (0, total - n * gw)))
        par = jnp.concatenate([row(0, 5, cw, 0), row(5, 6, gw, 0), row(6, 7, nw, 0), skip_row])
        head = jnp.pad(jnp.concatenate([h[:, :LANES] for h in heads]), ((0, 5), (0, 0)))
    layer, input_grad, grad_in, grad_out, dpar, dhead = device_part(
        tokens, cotangent, doc_lengths[0], in_full, out_full, par, head, n, dims
    )
    if direct:
        big_in, big_out, mine = reduce_call(grad_in.astype(BF), grad_out.astype(BF), dpar, dhead, n, dims)
    else:
        blocks = []
        for k in range(n):
            fit = lambda v, w: jnp.pad(v[:, k * w : (k + 1) * w], ((0, 0), (0, wide - w)))
            last = [jnp.pad(dhead[j : j + 1, k * hw : (k + 1) * hw], ((0, 0), (0, LANES - hw))) for j in range(3)]
            last = jnp.concatenate(last, axis=1)
            blocks.append(jnp.concatenate([
                fit(dpar[:5], cw), fit(dpar[5:6], gw), fit(dpar[6:7], nw),
                jnp.pad(last, ((0, 0), (0, wide - 3 * LANES))),
            ]).reshape(-1, LANES))
        unit = 2 * chips * 8
        packed = jnp.stack(blocks)
        size = packed.shape[1]
        packed = jnp.pad(packed, ((0, 0), (0, -size % unit), (0, 0))).reshape(-1, LANES)
        reduce = functools.partial(reduce_grad, core=core, me=me, n=n, chip=chip, chips=chips)
        big_out = reduce(grad_out, kind=BF)
        big_in = reduce(grad_in, kind=BF)
        mine = reduce(packed, kind=F32)[:size].reshape(8, wide)
    outs = [
        mine[0:4, :cw], mine[4, :cw], mine[7, :hw], mine[7, LANES : LANES + hw],
        mine[7, 2 * LANES : 2 * LANES + hw], mine[6, :nw], mine[5, :gw],
    ]
    return (layer, input_grad, big_in, big_out, *outs)


def solution(mesh):
    tok = P(("replica", "shard"), None)
    weights = (P("shard", None), P("shard", None), P(None, "shard")) + (P("shard"),) * 6
    return jax.shard_map(
        on_device,
        mesh=mesh,
        in_specs=(tok, tok, tok) + weights,
        out_specs=(tok, tok) + weights,
        check_vma=False,
    )
```

```python
import functools

import jax
import jax.numpy as jnp
from jax import lax
from jax.experimental import pallas as pl
from jax.experimental.pallas import tpu as pltpu
from jax.sharding import PartitionSpec as P

BLOCK = 256
LANES = 128
EPS = 1e-05
HIGH = lax.Precision.HIGHEST
BF = jnp.bfloat16
F32 = jnp.float32


def dot(a, b, dims=((1,), (0,)), precision=None):
    return lax.dot_general(a, b, (dims, ((), ())), preferred_element_type=F32, precision=precision)


def prenorm(values, gain_vec):
    scales = lax.rsqrt(jnp.mean(values * values, axis=1, keepdims=True) + EPS)
    return values * scales * gain_vec[None, :]


def three(v):
    hi = v.astype(BF)
    rest = v - hi.astype(F32)
    mid = rest.astype(BF)
    return hi, mid, (rest - mid.astype(F32)).astype(BF)


def exact_dot(m, v, dims=((1,), (0,))):
    hi, mid, lo = three(v)
    return dot(m, hi, dims) + (dot(m, mid, dims) + dot(m, lo, dims))


def bounds_of(len_ref):
    out, at = [], jnp.int32(0)
    for k in range(len_ref.shape[1]):
        at = at + len_ref[0, k]
        out.append(at)
    return out


def seg_of(places, bounds):
    seg = jnp.zeros(places.shape, jnp.int32)
    for b in bounds:
        seg = seg + (places >= b).astype(jnp.int32)
    return seg


def conv_pre(x_ref, par_ref, mask_ref, pad_s, taps_n):
    length = x_ref.shape[0]
    pad_s[0:8, :] = jnp.zeros((8, LANES), F32)
    pad_s[8 : 8 + length, :] = x_ref[...]
    pre = par_ref[taps_n : taps_n + 1, :] + par_ref[taps_n - 1 : taps_n, :] * x_ref[...]
    for k in range(1, taps_n):
        pre = pre + par_ref[taps_n - 1 - k : taps_n - k, :] * (
            pad_s[8 - k : 8 - k + length, :] * mask_ref[k - 1, 0:length, :]
        )
    return pre


def steps_in(raw_ref, head_ref, heads_all):
    lanes = lax.broadcasted_iota(jnp.int32, raw_ref.shape, 1) < heads_all
    raw = jnp.where(lanes, raw_ref[...] + head_ref[0:1, :], 0.0)
    lane = lax.broadcasted_iota(jnp.int32, (1, LANES), 1) < heads_all
    decays = jnp.where(lane, -jnp.exp(head_ref[1:2, :]), 0.0)
    spacing = jnp.where(lanes, jnp.maximum(raw, 0.0) + jnp.log(1.0 + jnp.exp(-jnp.abs(raw))), 0.0)
    return raw, decays, spacing, lanes


def prep_kernel(
    taps_n, block, heads_all, width,
    len_ref, b_ref, c_ref, raw_ref, pb_ref, pc_ref, head_ref,
    gram_ref, gramb_ref, gramt_ref, mask_ref, cols_ref, rows_ref, fac_ref,
    pad_s, cum_s,
):
    length = b_ref.shape[0]
    nb = length // block
    bounds = bounds_of(len_ref)
    places = lax.broadcasted_iota(jnp.int32, (length + 8, LANES), 0)
    seg = seg_of(places, bounds)
    for k in range(1, taps_n):
        ok = (places >= k) & (places < length) & (seg_of(places - k, bounds) == seg)
        mask_ref[k - 1] = jnp.where(ok, 1.0, 0.0)
    outs = []
    for x_ref, p_ref in ((b_ref, pb_ref), (c_ref, pc_ref)):
        pre = conv_pre(x_ref, p_ref, mask_ref, pad_s, taps_n)
        outs.append(pre * jax.nn.sigmoid(pre))
    keys, queries = outs
    kh = keys.astype(BF)
    kl = (keys - kh.astype(F32)).astype(BF)
    for i in range(nb):
        r = slice(i * block, (i + 1) * block)
        q = queries[r, :]
        qh = q.astype(BF)
        ql = (q - qh.astype(F32)).astype(BF)
        nt = ((1,), (1,))
        value = dot(qh, kh, nt) + (dot(qh, kl, nt) + dot(ql, kh, nt))
        row = lax.broadcasted_iota(jnp.int32, (block, length), 0) + i * block
        column = lax.broadcasted_iota(jnp.int32, (block, length), 1)
        same = (seg_of(row, bounds) == seg_of(column, bounds)) & (row >= column)
        value = jnp.where(same, value, 0.0)
        gram_ref[r, :] = value
        gramb_ref[r, :] = value.astype(BF)
        gramt_ref[:, r] = jnp.transpose(value).astype(BF)
    _, decays, spacing, _ = steps_in(raw_ref, head_ref, heads_all)
    lower = lax.broadcasted_iota(jnp.int32, (block, block), 0) >= lax.broadcasted_iota(jnp.int32, (block, block), 1)
    lower = jnp.where(lower, 1.0, 0.0).astype(BF)
    scaled = spacing * decays
    at = jnp.zeros((1, LANES), F32)
    starts, ends = [], []
    for i in range(nb):
        r = slice(i * block, (i + 1) * block)
        cum = exact_dot(lower, scaled[r, :]) + at
        cum_s[r, :] = cum
        starts.append(at)
        at = cum[block - 1 : block, :]
        ends.append(at)
        live = lax.broadcasted_iota(jnp.int32, (block, LANES), 1) < heads_all
        enter = jnp.where(live, jnp.exp(cum - starts[i]), 0.0)
        leave = jnp.where(live, jnp.exp(at - cum), 0.0)
        cols_ref[r, :] = (
            cum + pltpu.roll(spacing[r, :], heads_all, 1)
            + pltpu.roll(enter, 2 * heads_all, 1) + pltpu.roll(leave, 3 * heads_all, 1)
        )
    turned = jnp.transpose(cum_s[...])
    groups, heads = rows_ref.shape[0], rows_ref.shape[1]
    for g in range(groups):
        rows_ref[g] = turned[g * heads : (g + 1) * heads, :]
    facs = [jnp.exp(jnp.minimum(starts[i] - ends[j], 0.0)) for i in range(nb) for j in range(nb)]
    pad = fac_ref.shape[0] - len(facs)
    facs = jnp.concatenate(facs + [jnp.zeros((pad, LANES), F32)], axis=0)
    inner = fac_ref.shape[1]
    at_head = lax.broadcasted_iota(jnp.int32, (LANES, inner), 1) // width
    onehot = jnp.where(lax.broadcasted_iota(jnp.int32, (LANES, inner), 0) == at_head, 1.0, 0.0).astype(BF)
    hi, mid, lo = three(facs)
    fac_ref[...] = dot(hi, onehot) + (dot(mid, onehot) + dot(lo, onehot))


def side_specs(length, inner, state_at):
    col = lambda k: pl.BlockSpec((length, LANES), lambda i: (0, k))
    prow = lambda k: pl.BlockSpec((8, LANES), lambda i: (0, k))
    first = inner // LANES
    return [
        pl.BlockSpec(memory_space=pltpu.SMEM),
        col(2 * first), col(2 * first + 1), col(2 * first + 2),
        prow(first), prow(first + 1), pl.BlockSpec((8, LANES), lambda i: (0, 0)),
    ]


def whole(*shape):
    return pl.BlockSpec(shape, lambda i: (0,) * len(shape))


def prep_call(lengths, projected, par, head, inner, taps_n, heads_all):
    length = projected.shape[0]
    width = inner // heads_all
    groups, heads = inner // LANES, LANES // width
    nb = length // BLOCK
    shapes = [
        ((length, length), F32), ((length, length), BF), ((length, length), BF),
        ((taps_n - 1, length + 8, LANES), F32), ((length, LANES), F32),
        ((groups, heads, length), F32), ((-(-nb * nb // 8) * 8, inner), F32),
    ]
    return pl.pallas_call(
        functools.partial(prep_kernel, taps_n, BLOCK, heads_all, width),
        grid=(1,),
        in_specs=side_specs(length, inner, heads_all),
        out_specs=[whole(*s) for s, _ in shapes],
        out_shape=[jax.ShapeDtypeStruct(s, d) for s, d in shapes],
        scratch_shapes=[pltpu.VMEM((length + 8, LANES), F32), pltpu.VMEM((length, LANES), F32)],
        compiler_params=pltpu.CompilerParams(vmem_limit_bytes=48 * 1024 * 1024),
        cost_estimate=pl.CostEstimate(
            flops=8 * length * length * LANES, bytes_accessed=16 * length * length, transcendentals=0
        ),
    )(lengths, projected, projected, projected, par, par, head)


def post_kernel(
    taps_n, block, heads_all,
    len_ref, b_ref, c_ref, raw_ref, pb_ref, pc_ref, head_ref, mask_ref, dgram_ref, dc_ref, ddt_ref,
    db_ref, dcc_ref, draw_ref, sb_ref, sc_ref, dhead_ref,
    pad_s, dpad_s,
):
    length = b_ref.shape[0]
    nb = length // block
    bounds = bounds_of(len_ref)
    total = lambda v: jnp.sum(v, axis=0, keepdims=True)
    sig, act = [], []
    for x_ref, p_ref in ((b_ref, pb_ref), (c_ref, pc_ref)):
        pre = conv_pre(x_ref, p_ref, mask_ref, pad_s, taps_n)
        sg = jax.nn.sigmoid(pre)
        sig.append(sg)
        act.append(pre * sg)
    kb = act[0].astype(BF)
    qt = jnp.transpose(act[1]).astype(BF)
    dkt = jnp.zeros((LANES, length), F32)
    dq = []
    for i in range(nb):
        r = slice(i * block, (i + 1) * block)
        row = lax.broadcasted_iota(jnp.int32, (block, length), 0) + i * block
        column = lax.broadcasted_iota(jnp.int32, (block, length), 1)
        same = (seg_of(row, bounds) == seg_of(column, bounds)) & (row >= column)
        d = jnp.where(same, dgram_ref[r, :], 0.0).astype(BF)
        dq.append(dot(d, kb))
        dkt = dkt + dot(qt[:, r], d)
    grads = (jnp.transpose(dkt), jnp.concatenate(dq, axis=0))
    dpad_s[length : length + 8, :] = jnp.zeros((8, LANES), F32)
    for n, (x_ref, p_ref, o_ref, s_ref) in enumerate(
        ((b_ref, pb_ref, db_ref, sb_ref), (c_ref, pc_ref, dcc_ref, sc_ref))
    ):
        dpre = grads[n] * (sig[n] + act[n] * (1.0 - sig[n]))
        dpad_s[0:length, :] = dpre
        pad_s[8 : 8 + length, :] = x_ref[...]
        out = p_ref[taps_n - 1 : taps_n, :] * dpre
        sums = [None] * (taps_n - 1) + [total(dpre * x_ref[...]), total(dpre)]
        for k in range(1, taps_n):
            out = out + p_ref[taps_n - 1 - k : taps_n - k, :] * (
                dpad_s[k : k + length, :] * mask_ref[k - 1, k : k + length, :]
            )
            sums[taps_n - 1 - k] = total(
                dpre * mask_ref[k - 1, 0:length, :] * pad_s[8 - k : 8 - k + length, :]
            )
        o_ref[...] = out.astype(BF)
        s_ref[...] = jnp.concatenate(sums + [jnp.zeros((7 - taps_n, LANES), F32)], axis=0)
    raw, decays, spacing, lanes = steps_in(raw_ref, head_ref, heads_all)
    upper = lax.broadcasted_iota(jnp.int32, (block, block), 0) <= lax.broadcasted_iota(jnp.int32, (block, block), 1)
    upper = jnp.where(upper, 1.0, 0.0).astype(BF)
    at = jnp.zeros((1, LANES), F32)
    d_shift, d_logs = jnp.zeros((1, LANES), F32), jnp.zeros((1, LANES), F32)
    for i in reversed(range(nb)):
        r = slice(i * block, (i + 1) * block)
        back = exact_dot(upper, dc_ref[r, :]) + at
        at = back[0:1, :]
        d_logs = d_logs + total(spacing[r, :] * back)
        d_raw = jnp.where(lanes[r, :], (ddt_ref[r, :] + decays * back) * jax.nn.sigmoid(raw[r, :]), 0.0)
        d_shift = d_shift + total(d_raw)
        draw_ref[r, :] = d_raw.astype(BF)
    dhead_ref[...] = jnp.concatenate([d_shift, d_logs * decays, jnp.zeros((6, LANES), F32)], axis=0)


def post_call(lengths, projected, par, head, masks, dgram, dcum, dspacing, inner, taps_n, heads_all):
    length = projected.shape[0]
    shapes = [
        ((length, LANES), BF), ((length, LANES), BF), ((length, LANES), BF),
        ((8, LANES), F32), ((8, LANES), F32), ((8, LANES), F32),
    ]
    return pl.pallas_call(
        functools.partial(post_kernel, taps_n, BLOCK, heads_all),
        grid=(1,),
        in_specs=side_specs(length, inner, heads_all) + [whole(*v.shape) for v in (masks, dgram, dcum, dspacing)],
        out_specs=[whole(*s) for s, _ in shapes],
        out_shape=[jax.ShapeDtypeStruct(s, d) for s, d in shapes],
        scratch_shapes=[pltpu.VMEM((length + 8, LANES), F32), pltpu.VMEM((length + 8, LANES), F32)],
        compiler_params=pltpu.CompilerParams(vmem_limit_bytes=48 * 1024 * 1024),
        cost_estimate=pl.CostEstimate(
            flops=4 * length * length * LANES, bytes_accessed=8 * length * length, transcendentals=0
        ),
    )(lengths, projected, projected, projected, par, par, head, masks, dgram, dcum, dspacing)


def mixer_kernel(
    inner, taps_n, block, width,
    z_ref, cin_ref, gm_ref, par_ref, mask_ref, gram_ref, gramb_ref, gramt_ref,
    rows_ref, pack_ref, fac_ref,
    dz_ref, dcin_ref, mixed_ref, dgram_ref, dc_ref, ddt_ref, sums_ref,
    pre_s, sp_s, sz_s, ub_s, yd_s, yo_s, mix_s, ss_s, q_s, pad_s, dpad_s, cols_s,
):
    phase, g = pl.program_id(0), pl.program_id(1)
    taps_ref = par_ref.at[0:4]
    bias_ref, gain_ref, skip_ref = par_ref.at[4:5], par_ref.at[5:6], par_ref.at[7:8]
    length = z_ref.shape[0]
    nb = length // block
    heads = LANES // width
    heads_all = inner // width
    half = block // 2

    def col(k, rows):
        parts = [
            jnp.broadcast_to(cols_s[rows, k * heads_all + h : k * heads_all + h + 1], (block, width))
            for h in range(heads)
        ]
        return jnp.concatenate(parts, axis=1)

    blocks = [slice(i * block, (i + 1) * block) for i in range(nb)]
    up = lambda v: v.astype(F32)

    def decay_of(h, r0, r1, c0, c1):
        spread = cols_s[r0:r1, h : h + 1] - rows_ref[0, h : h + 1, c0:c1]
        return jnp.exp(jnp.minimum(spread, 0.0))

    @pl.when((phase == 0) & (g == 0))
    def _():
        ss_s[...] = jnp.zeros_like(ss_s)
        q_s[...] = jnp.zeros_like(q_s)
        dgram_ref[...] = jnp.zeros_like(dgram_ref)
        dc_ref[...] = jnp.zeros_like(dc_ref)
        ddt_ref[...] = jnp.zeros_like(ddt_ref)
        pad_s[0:8, :] = jnp.zeros((8, LANES), F32)
        dpad_s[length : length + 8, :] = jnp.zeros((8, LANES), F32)

    pad_s[8 : 8 + length, :] = cin_ref[...]
    cols_s[...] = pltpu.roll(pack_ref[...], lax.rem(LANES - g * heads, LANES), 1)

    @pl.when(phase == 0)
    def _():
        vs = []
        for i in range(nb):
            r = blocks[i]
            r0, rm, r1 = i * block, i * block + half, (i + 1) * block
            p_r = bias_ref[0:1, :] + taps_ref[taps_n - 1 : taps_n, :] * cin_ref[r, :]
            for k in range(1, taps_n):
                p_r = p_r + taps_ref[taps_n - 1 - k : taps_n - k, :] * (
                    pad_s[8 - k + r0 : 8 - k + r1, :] * mask_ref[k - 1, r0:r1, :]
                )
            pre_s[g, r, :] = p_r
            sp = jax.nn.sigmoid(p_r)
            sp_s[g, r, :] = sp
            x = p_r * sp
            u = x * col(1, r)
            ub = u.astype(BF)
            ub_s[g, r, :] = ub
            vs.append((up(ub) * col(3, r)).astype(BF))
            tops, bots = [], []
            for h in range(heads):
                lanes = slice(h * width, (h + 1) * width)
                top = (decay_of(h, r0, rm, r0, rm) * gram_ref[r0:rm, r0:rm]).astype(BF)
                bot = (decay_of(h, rm, r1, r0, r1) * gram_ref[rm:r1, r0:r1]).astype(BF)
                mix_s[g, h, i, 0:half, 0:half] = top
                mix_s[g, h, i, half:block, :] = bot
                tops.append(dot(top, ub[0:half, lanes]))
                bots.append(dot(bot, ub[:, lanes]))
            yd = jnp.concatenate([jnp.concatenate(tops, axis=1), jnp.concatenate(bots, axis=1)], axis=0)
            yd_s[g, r, :] = yd
            y = yd + skip_ref[0:1, :] * x
            if i:
                yo = jnp.zeros((block, LANES), F32)
                for j in range(i):
                    yo = yo + dot(gramb_ref[r, blocks[j]], vs[j]) * fac_ref[i * nb + j : i * nb + j + 1, :]
                yo_s[g, r, :] = yo
                y = y + yo * col(2, r)
            z = z_ref[r, :]
            sz = jax.nn.sigmoid(z)
            sz_s[g, r, :] = sz
            gated = y * (z * sz)
            ss_s[r, :] += gated * gated
            q_s[r, :] += gm_ref[r, :] * gain_ref[0:1, :] * gated

    @pl.when((phase == 1) & (g == 0))
    def _():
        scale = lax.rsqrt(jnp.sum(ss_s[...], axis=1, keepdims=True) / inner + EPS)
        coef = jnp.sum(q_s[...], axis=1, keepdims=True) * scale * scale * scale / inner
        ss_s[...] = jnp.broadcast_to(scale, ss_s.shape)
        q_s[...] = jnp.broadcast_to(coef, q_s.shape)

    @pl.when(phase == 1)
    def _():
        lane = lax.broadcasted_iota(jnp.int32, (LANES, LANES), 0) // width
        target = lax.broadcasted_iota(jnp.int32, (LANES, LANES), 1)
        pick = jnp.where(lane + g * heads == target, 1.0, 0.0).astype(BF)

        def by_head(d):
            hi = d.astype(BF)
            lo = (d - hi.astype(F32)).astype(BF)
            return dot(hi, pick) + dot(lo, pick)

        ws = []
        dskip = jnp.zeros((1, LANES), F32)
        dgain = jnp.zeros((1, LANES), F32)
        for i in range(nb):
            r = blocks[i]
            x = pre_s[g, r, :] * sp_s[g, r, :]
            z = z_ref[r, :]
            sig = sz_s[g, r, :]
            act = z * sig
            y = yd_s[g, r, :] + skip_ref[0:1, :] * x
            if i:
                a = col(2, r)
                y = y + yo_s[g, r, :] * a
            gated = y * act
            normal = gated * ss_s[r, :]
            mixed_ref[r, :] = (normal * gain_ref[0:1, :]).astype(BF)
            gm = gm_ref[r, :]
            dgain = dgain + jnp.sum(gm * normal, axis=0, keepdims=True)
            dgated = gm * gain_ref[0:1, :] * ss_s[r, :] - gated * q_s[r, :]
            dz_ref[r, :] = (dgated * y * (sig + act * (1.0 - sig))).astype(BF)
            dy = dgated * act
            dskip = dskip + jnp.sum(dy * x, axis=0, keepdims=True)
            dpad_s[r, :] = dy
            ws.append((dy * a).astype(BF) if i else None)
        for j in range(nb):
            r = blocks[j]
            r0, rm, r1 = j * block, j * block + half, (j + 1) * block
            dy = dpad_s[r, :]
            dyb = dy.astype(BF)
            dyt = jnp.transpose(dy).astype(BF)
            ub = ub_s[g, r, :]
            dut = []
            tops, bots = jnp.zeros((half, half), F32), jnp.zeros((half, block), F32)
            for h in range(heads):
                lanes = slice(h * width, (h + 1) * width)
                left = dot(dyt[lanes, :], mix_s[g, h, j, :, 0:half])
                right = dot(dyt[lanes, half:block], mix_s[g, h, j, half:block, half:block])
                dut.append(jnp.concatenate([left, right], axis=1))
                tops = tops + decay_of(h, r0, rm, r0, rm) * dot(
                    dyb[0:half, lanes], ub[0:half, lanes], ((1,), (1,))
                )
                bots = bots + decay_of(h, rm, r1, r0, r1) * dot(
                    dyb[half:block, lanes], ub[:, lanes], ((1,), (1,))
                )
            dgram_ref[r0:rm, r0:rm] += tops
            dgram_ref[rm:r1, r0:r1] += bots
            du = jnp.transpose(jnp.concatenate(dut, axis=0))
            uf = up(ub)
            dcum = up(dyb) * yd_s[g, r, :] - uf * du
            if j:
                dcum = dcum + up(ws[j]) * yo_s[g, r, :]
            if j < nb - 1:
                leave = col(3, r)
                v = (uf * leave).astype(BF)
                dv = jnp.zeros((block, LANES), F32)
                for i in range(j + 1, nb):
                    fac = fac_ref[i * nb + j : i * nb + j + 1, :]
                    dv = dv + dot(gramt_ref[r, blocks[i]], ws[i]) * fac
                    dgram_ref[blocks[i], r] += dot((up(ws[i]) * fac).astype(BF), v, ((1,), (1,)))
                dcum = dcum - up(v) * dv
                du = du + dv * leave
            dc_ref[r, :] += by_head(dcum)
            sig = sp_s[g, r, :]
            x = pre_s[g, r, :] * sig
            ddt_ref[r, :] += by_head(du * x)
            dx = skip_ref[0:1, :] * dy + du * col(1, r)
            dpad_s[r, :] = dx * (sig + x * (1.0 - sig))
        acc = [jnp.zeros((1, LANES), F32) for _ in range(taps_n + 1)]
        total = lambda v: jnp.sum(v, axis=0, keepdims=True)
        for i in range(nb):
            r0, r1 = i * block, (i + 1) * block
            dpre = dpad_s[r0:r1, :]
            dcin = taps_ref[taps_n - 1 : taps_n, :] * dpre
            acc[taps_n - 1] = acc[taps_n - 1] + total(dpre * cin_ref[r0:r1, :])
            acc[taps_n] = acc[taps_n] + total(dpre)
            for k in range(1, taps_n):
                dcin = dcin + taps_ref[taps_n - 1 - k : taps_n - k, :] * (
                    dpad_s[r0 + k : r1 + k, :] * mask_ref[k - 1, r0 + k : r1 + k, :]
                )
                acc[taps_n - 1 - k] = acc[taps_n - 1 - k] + total(
                    dpre * mask_ref[k - 1, r0:r1, :] * pad_s[8 - k + r0 : 8 - k + r1, :]
                )
            dcin_ref[r0:r1, :] = dcin.astype(BF)
        sums_ref[...] = jnp.concatenate(acc + [dgain, dskip, jnp.zeros((1, LANES), F32)], axis=0)


def mixer_call(projected, gm, par, inner, taps_n, sides, heads_all):
    length = projected.shape[0]
    width = inner // heads_all
    heads = LANES // width
    groups = inner // LANES
    block = BLOCK
    nb = length // block
    gram, gram_b, gram_t, masks, cols, rows, fac = sides
    n_sum = 8

    part = lambda off: pl.BlockSpec((length, LANES), lambda p, g: (0, off + g))
    row = lambda n: pl.BlockSpec((n, LANES), lambda p, g: (0, g))
    full = lambda *s: pl.BlockSpec(s, lambda p, g: (0,) * len(s))
    late = lambda n: pl.BlockSpec((n, LANES), lambda p, g: (0, p * g))
    sds = jax.ShapeDtypeStruct
    return pl.pallas_call(
        functools.partial(mixer_kernel, inner, taps_n, block, width),
        grid=(2, groups),
        in_specs=[
            part(0), part(groups), part(0), row(8),
            full(taps_n - 1, length + 8, LANES), full(length, length),
            full(length, length), full(length, length),
            pl.BlockSpec((1, heads, length), lambda p, g: (g, 0, 0)),
            full(length, LANES),
            row(fac.shape[0]),
        ],
        out_specs=[
            late(length), late(length), late(length), full(length, length),
            full(length, LANES), full(length, LANES), late(n_sum),
        ],
        out_shape=[
            sds((length, inner), BF), sds((length, inner), BF), sds((length, inner), BF),
            sds((length, length), F32), sds((length, LANES), F32), sds((length, LANES), F32),
            sds((n_sum, inner), F32),
        ],
        scratch_shapes=[
            pltpu.VMEM((groups, length, LANES), F32),
            pltpu.VMEM((groups, length, LANES), F32),
            pltpu.VMEM((groups, length, LANES), F32),
            pltpu.VMEM((groups, length, LANES), BF),
            pltpu.VMEM((groups, length, LANES), F32),
            pltpu.VMEM((groups, length, LANES), F32),
            pltpu.VMEM((groups, heads, nb, block, block), BF),
            pltpu.VMEM((length, LANES), F32),
            pltpu.VMEM((length, LANES), F32),
            pltpu.VMEM((length + 8, LANES), F32),
            pltpu.VMEM((length + 8, LANES), F32),
            pltpu.VMEM((length, LANES), F32),
        ],
        compiler_params=pltpu.CompilerParams(
            vmem_limit_bytes=60 * 1024 * 1024, dimension_semantics=("arbitrary", "arbitrary")
        ),
        cost_estimate=pl.CostEstimate(
            flops=20 * length * block * inner, bytes_accessed=40 * length * inner, transcendentals=0
        ),
    )(
        projected, projected, gm, par, masks, gram, gram_b, gram_t, rows, cols, fac,
    )


def device_part(tokens, cotangent, lengths, in_full, out_full, par, head, n, dims):
    cw, gw, nw, hw = dims
    length = tokens.shape[0]
    inner, channels, heads_all = n * gw, n * cw, n * hw
    taps_n = 4
    valid = jnp.arange(length, dtype=jnp.int32) < jnp.sum(lengths)
    gain_vec = par[6, : n * nw]
    values = tokens.astype(F32)
    normed = prenorm(values, gain_vec).astype(BF)
    projected = dot(normed, in_full)
    masked = cotangent * valid.astype(BF)[:, None]
    grad_mixed = dot(masked, out_full, ((1,), (1,)))
    sides = prep_call(lengths, projected, par, head, inner, taps_n, heads_all)
    dz, dcin, mixed, dgram, dcum, dspacing, sums = mixer_call(
        projected, grad_mixed, par, inner, taps_n, sides, heads_all
    )
    grad_outw = dot(mixed, masked, ((0,), (0,)))
    db, dc, draw, sums_b, sums_c, dhead = post_call(
        lengths, projected, par, head, sides[3], dgram, dcum, dspacing, inner, taps_n, heads_all
    )
    d_skip = jnp.sum(sums[6].reshape(heads_all, -1), axis=1)
    grad_proj = jnp.concatenate([dz, dcin, db, dc, draw[:, :heads_all]], axis=1)
    layer = values + valid.astype(F32)[:, None] * dot(mixed, out_full)
    grad_normed = dot(grad_proj, in_full, ((1,), (1,)))
    _, norm_back = jax.vjp(prenorm, values, gain_vec)
    grad_norm_in, grad_gain = norm_back(grad_normed)
    input_grad = cotangent.astype(F32) + grad_norm_in
    fit = lambda v, w: jnp.pad(v, ((0, 0), (0, w - v.shape[1])))
    dpar = jnp.concatenate([
        jnp.concatenate([sums[:5], sums_b[:5], sums_c[:5]], axis=1),
        fit(sums[5:6], channels), fit(grad_gain[None], channels), jnp.zeros((1, channels), F32),
    ])
    dhead = dhead + jnp.pad(d_skip[None], ((2, 5), (0, LANES - heads_all)))
    return layer, input_grad, normed, grad_proj, grad_outw, dpar, dhead


def moved(x, step):
    n_rep, n = lax.axis_size("replica"), lax.axis_size("shard")
    perm = []
    for r in range(n_rep):
        for s in range(n):
            to_r, to_s = step(r, s)
            perm.append((r * n + s, to_r * n + to_s))
    return lax.ppermute(x, ("replica", "shard"), perm)


def pick(x, i):
    return lax.dynamic_index_in_dim(x, i, 0, keepdims=False)


def ring_all(x, index, n, step):
    got = jnp.stack([x] + [moved(x, functools.partial(step, k)) for k in range(1, n)])
    return jnp.stack([pick(got, lax.rem(index - j + n, n)) for j in range(n)])


def ring_sum(parts, index, n, step):
    total = pick(parts, index).astype(F32)
    for k in range(1, n):
        total = total + moved(pick(parts, lax.rem(index + k, n)), functools.partial(step, k))
    return total


def shard_step(k, r, s):
    return r, (s + k) % lax.axis_size("shard")


def chip_step(k, r, s):
    return (r + 2 * k) % lax.axis_size("replica"), s


def core_step(r, s):
    return r ^ 1, s


def both_halves(mine, core, axis):
    other = moved(mine, core_step)
    first = jnp.where(core == 0, mine, other)
    second = jnp.where(core == 0, other, mine)
    return jnp.stack([first, second], axis=axis)


def gather_weight(shard, core, me, n):
    half = pick(shard.reshape(2, -1, shard.shape[1]), core)
    mine = ring_all(half, me, n, shard_step)
    return both_halves(mine, core, 1).reshape(-1, shard.shape[1])


def reduce_grad(grad, core, me, n, chip, chips, kind):
    columns = grad.shape[1]
    blocks = grad.astype(kind).reshape(n, 2, -1, columns)
    keep = lax.dynamic_index_in_dim(blocks, core, 1, keepdims=False)
    send = lax.dynamic_index_in_dim(blocks, 1 - core, 1, keepdims=False)
    pair = (keep.astype(F32) + moved(send, core_step).astype(F32)).astype(kind)
    mine = ring_sum(pair, me, n, shard_step).astype(kind)
    piece = ring_sum(mine.reshape(chips, -1, columns), chip, chips, chip_step).astype(kind)
    half = ring_all(piece, chip, chips, chip_step).reshape(-1, columns)
    return both_halves(half, core, 0).reshape(-1, columns).astype(F32)


MESH = pl.DeviceIdType.MESH


def peers():
    rep, s = lax.axis_index("replica"), lax.axis_index("shard")
    return rep, s


def flip(v, bit):
    return v + bit - 2 * bit * lax.rem(lax.div(v, bit), 2)


def greet(targets):
    barrier = pltpu.get_barrier_semaphore()
    for t in targets:
        pl.semaphore_signal(barrier, inc=1, device_id=t, device_id_type=MESH)
    pl.semaphore_wait(barrier, len(targets))


def join_rows(parts, width, total):
    have = parts[0].shape[1]
    acc = None
    for k, v in enumerate(parts):
        if have < total:
            v = jnp.concatenate([v, jnp.zeros((v.shape[0], total - have), v.dtype)], axis=1)
        elif have > total:
            v = v[:, :total]
        v = v if k == 0 else pltpu.roll(v, k * width, 1)
        acc = v if acc is None else acc + v
    return acc


def gather_kernel(
    dims, win_ref, wout_ref, small_ref, in_ref, out_ref, par_ref, head_ref,
    small_all, send_sem, recv_sem, local_sem,
):
    cw, gw, nw, hw = dims
    rep, s = peers()
    core, z = lax.rem(rep, 2), lax.div(rep, 2)
    par = lax.rem(z, 2)
    x_s, y_s, d_s = flip(s, 1), flip(s, 2), flip(flip(s, 1), 2)
    core_r, z_r = flip(rep, 1), flip(rep, 2)
    greet([(rep, x_s), (rep, y_s), (rep, d_s), (core_r, s), (z_r, s)])
    made = []

    def send(src, dst, to):
        k = len(made)
        c = pltpu.make_async_remote_copy(
            src_ref=src, dst_ref=dst, send_sem=send_sem.at[k], recv_sem=recv_sem.at[k],
            device_id=to, device_id_type=MESH,
        )
        c.start()
        made.append(c)
        return c

    smalls = [send(small_ref, small_all.at[s], (rep, to)) for to in (x_s, y_s, d_s)]
    small_own = pltpu.make_async_copy(small_ref, small_all.at[s], local_sem.at[2])
    small_own.start()
    locals_ = [small_own]
    arrays = [(win_ref, in_ref), (wout_ref, out_ref)]

    def rows(a, c, q, h):
        half = arrays[a][0].shape[0] // 2
        sixth = half // 6
        return pl.ds(pl.multiple_of(c * half + q * (2 * sixth) + h * sixth, sixth), sixth)

    own, other = 2 * par, 2 - 2 * par
    first = {}
    for q in (own, 1):
        qk = "s" if isinstance(q, int) else "o"
        for a in (1, 0):
            src, dst = arrays[a]
            for h in (0, 1):
                r = rows(a, core, q, h)
                order = ((x_s, "x"), (y_s, "y")) if h == 0 else ((y_s, "y"), (x_s, "x"))
                for to, name in order:
                    first[qk, a, h, name] = send(src.at[r], dst.at[s, r], (rep, to))
    for a in (0, 1):
        src, dst = arrays[a]
        c = pltpu.make_async_copy(src, dst.at[s], local_sem.at[a])
        c.start()
        locals_.append(c)

    relay, over_z, over_core = {}, [], []

    def spread(a, sh, q, h, up):
        dst = arrays[a][1]
        r = rows(a, core, q, h)
        if up:
            over_z.append((a, sh, h, send(dst.at[sh, r], dst.at[sh, r], (z_r, s))))
        over_core.append(send(dst.at[sh, r], dst.at[sh, r], (core_r, s)))

    for q in (own, 1):
        qk = "s" if isinstance(q, int) else "o"
        for a in (1, 0):
            dst = arrays[a][1]
            for h in (0, 1):
                r = rows(a, core, q, h)
                order = ((x_s, "x"), (y_s, "y")) if h == 0 else ((y_s, "y"), (x_s, "x"))
                for sh, name in order:
                    first[qk, a, h, name].wait_recv()
                    if (name == "x") == (h == 0):
                        to = y_s if h == 0 else x_s
                        relay[qk, a, h] = send(dst.at[sh, r], dst.at[sh, r], (rep, to))
                    spread(a, sh, q, h, qk == "o")
        if qk == "o":
            for c in smalls:
                c.wait_recv()
            small_own.wait()
            n = small_all.shape[0]
            total = par_ref.shape[1]
            taken = lambda lo, hi: [small_all[k, lo:hi, :] for k in range(n)]
            par_ref[0:5, :] = join_rows(taken(0, 5), cw, total)
            par_ref[5:6, :] = join_rows(taken(5, 6), gw, total)
            par_ref[6:7, :] = join_rows(taken(6, 7), nw, total)
            heads = [
                join_rows([small_all[k, 7:8, j * LANES : (j + 1) * LANES] for k in range(n)], hw, LANES)
                for j in range(3)
            ]
            head_ref[...] = jnp.concatenate(heads + [jnp.zeros((5, LANES), F32)], axis=0)
            lane_head = lax.broadcasted_iota(jnp.int32, (LANES, total), 1) // (gw // hw)
            pick_m = jnp.where(lax.broadcasted_iota(jnp.int32, (LANES, total), 0) == lane_head, 1.0, 0.0)
            wide = lax.dot_general(
                jnp.broadcast_to(heads[2], (8, LANES)), pick_m, (((1,), (0,)), ((), ())),
                preferred_element_type=F32, precision=HIGH,
            )
            par_ref[7:8, :] = wide[0:1, :]
    for q in (own, 1):
        qk = "s" if isinstance(q, int) else "o"
        for a in (1, 0):
            for h in (0, 1):
                relay[qk, a, h].wait_recv()
                spread(a, d_s, q, h, qk == "o")
    for a, sh, h, c in list(over_z):
        c.wait_recv()
        spread(a, sh, other, h, False)
    for c in over_core:
        c.wait_recv()
    for c in locals_[1:]:
        c.wait()
    for c in made:
        c.wait_send()


def gather_call(w_in, w_out, small, n, dims):
    cw, gw, nw, hw = dims
    sds = jax.ShapeDtypeStruct
    vm, anyw = pl.BlockSpec(memory_space=pltpu.VMEM), pl.BlockSpec(memory_space=pl.ANY)
    copies = 96
    full_in, full_out, par, head = pl.pallas_call(
        functools.partial(gather_kernel, dims),
        in_specs=[vm, vm, vm],
        out_specs=[anyw, anyw, vm, vm],
        out_shape=[
            sds((n, *w_in.shape), BF), sds((n, *w_out.shape), BF),
            sds((8, -(-cw * n // LANES) * LANES), F32), sds((8, LANES), F32),
        ],
        scratch_shapes=[
            pltpu.VMEM((n, *small.shape), F32),
            pltpu.SemaphoreType.DMA((copies,)),
            pltpu.SemaphoreType.DMA((copies,)),
            pltpu.SemaphoreType.DMA((3,)),
        ],
        compiler_params=pltpu.CompilerParams(
            collective_id=0, has_side_effects=True, vmem_limit_bytes=40 * 1024 * 1024
        ),
    )(w_in, w_out, small)
    return full_in.reshape(-1, w_in.shape[1]), full_out.reshape(-1, w_out.shape[1]), par, head


def reduce_kernel(
    dims, lead, normed_ref, gp_ref, gout_ref, dpar_ref, dhead_ref, fin_ref, fout_ref, fs_ref,
    pin, pout, psm, bin1, bout1, bsm1, bin2, bout2, bsm2, cin, cout, csm, tin, tout,
    gin_ref, turned, send_sem, recv_sem,
):
    cw, gw, nw, hw = dims
    rep, s = peers()
    core, z = lax.rem(rep, 2), lax.div(rep, 2)
    mid = (z == 1) | (z == 2)
    x_s, y_s, d_s = flip(s, 1), flip(s, 2), flip(flip(s, 1), 2)
    core_r, pair_r, mid_r = flip(rep, 1), flip(rep, 2), (3 - z) * 2 + core
    n = psm.shape[0]
    count = [0]

    def remote(src, dst, to):
        k = count[0]
        count[0] += 1
        return pltpu.make_async_remote_copy(
            src_ref=src, dst_ref=dst, send_sem=send_sem.at[k], recv_sem=recv_sem.at[k],
            device_id=to, device_id_type=MESH,
        )

    big = [
        (gin_ref, fin_ref, pin, bin1, bin2, cin, tin),
        (gout_ref, fout_ref, pout, bout1, bout2, cout, tout),
    ]

    def piece(a, k, rows, alpha):
        g, fin, p, b1, b2, c, t = big[a]
        half = p.shape[1]
        r = pl.ds(k * rows, rows)
        mine = pl.ds(pl.multiple_of(core * half + k * rows, rows), rows)
        theirs = pl.ds(pl.multiple_of((1 - core) * half + k * rows, rows), rows)
        one, two = (x_s, y_s) if alpha else (y_s, x_s)
        up = lambda v: v.astype(F32)
        st = {}

        def s0():
            st["a"] = remote(g.at[:, theirs], p.at[:, r], (core_r, s))
            st["a"].start()

        def s1():
            st["a"].wait_recv()
            for sh in (one, d_s):
                p[sh, r] = (up(p[sh, r]) + up(g[sh, mine])).astype(BF)
            st["b0"] = remote(p.at[d_s, r], b1.at[1, r], (rep, one))
            st["b0"].start()
            st["b1"] = remote(p.at[one, r], b1.at[0, r], (rep, one))
            st["b1"].start()

        def s2():
            st["b0"].wait_recv()
            p[two, r] = (up(p[two, r]) + up(g[two, mine]) + up(b1[1, r])).astype(BF)
            st["c"] = remote(p.at[two, r], b2.at[r], (rep, two))
            st["c"].start()

        def s3():
            st["b1"].wait_recv()
            st["c"].wait_recv()
            total = up(p[s, r]) + up(g[s, mine]) + up(b1[0, r]) + up(b2[r])
            p[s, r] = total.astype(BF)
            st["z1"] = remote(p.at[s, r], c.at[0, r], (pair_r, s))

            @pl.when(jnp.logical_not(mid))
            def _():
                st["z1"].start()

        def s4():
            st["z2"] = remote(t.at[r], c.at[1, r], (mid_r, s))

            @pl.when(mid)
            def _():
                st["z1"].wait_recv()
                t[r] = (up(p[s, r]) + up(c[0, r])).astype(BF)
                st["z2"].start()

        def s5():
            st["z3"] = remote(fin.at[core, r], fin.at[core, r], (pair_r, s))
            st["f"] = remote(fin.at[core, r], fin.at[core, r], (core_r, s))

            @pl.when(mid)
            def _():
                st["z2"].wait_recv()
                fin[core, r] = (up(t[r]) + up(c[1, r])).astype(BF)
                st["z3"].start()
                st["f"].start()

        def s6():
            @pl.when(jnp.logical_not(mid))
            def _():
                st["z3"].wait_recv()
                st["f"].start()

        def s7():
            st["f"].wait_recv()
            st["f"].wait_send()
            for name in ("a", "b0", "b1", "c"):
                st[name].wait_send()

            @pl.when(mid)
            def _():
                st["z2"].wait_send()
                st["z3"].wait_send()

            @pl.when(jnp.logical_not(mid))
            def _():
                st["z1"].wait_send()

        return [s0, s1, s2, s3, s4, s5, s6, s7]

    def small_piece():
        st = {}

        def s0():
            dpar, dh = dpar_ref[...], dhead_ref[...]
            wide = fs_ref.shape[1]
            back = lambda v, k: (v if k == 0 else pltpu.roll(v, v.shape[1] - k, 1))
            for k in range(n):
                head = back(dh, k * hw)
                row = jnp.concatenate([head[j : j + 1, :] for j in range(3)], axis=1)
                if wide > 3 * LANES:
                    row = jnp.concatenate([row, jnp.zeros((1, wide - 3 * LANES), F32)], axis=1)
                csm[2 + k] = jnp.concatenate(
                    [
                        back(dpar, k * cw)[0:5, :wide], back(dpar, k * gw)[5:6, :wide],
                        back(dpar, k * nw)[6:7, :wide], row,
                    ],
                    axis=0,
                )
            st["a"] = remote(csm.at[pl.ds(2, n)], psm, (core_r, s))
            st["a"].start()

        def s1():
            st["a"].wait_recv()
            for k in range(n):
                psm[k] = psm[k] + csm[2 + k]
            st["b0"] = remote(psm.at[d_s], bsm1.at[1], (rep, x_s))
            st["b0"].start()
            st["b1"] = remote(psm.at[x_s], bsm1.at[0], (rep, x_s))
            st["b1"].start()

        def s2():
            st["b0"].wait_recv()
            psm[y_s] = psm[y_s] + bsm1[1]
            st["c"] = remote(psm.at[y_s], bsm2, (rep, y_s))
            st["c"].start()

        def s3():
            st["b1"].wait_recv()
            st["c"].wait_recv()
            psm[s] = psm[s] + bsm1[0] + bsm2[...]
            st["z1"] = remote(psm.at[s], csm.at[0], (pair_r, s))

            @pl.when(jnp.logical_not(mid))
            def _():
                st["z1"].start()

        def s4():
            st["z2"] = remote(bsm1.at[2], csm.at[1], (mid_r, s))

            @pl.when(mid)
            def _():
                st["z1"].wait_recv()
                bsm1[2] = psm[s] + csm[0]
                st["z2"].start()

        def s5():
            st["z3"] = remote(fs_ref, fs_ref, (pair_r, s))

            @pl.when(mid)
            def _():
                st["z2"].wait_recv()
                fs_ref[...] = bsm1[2] + csm[1]
                st["z3"].start()

        def s6():
            @pl.when(jnp.logical_not(mid))
            def _():
                st["z3"].wait_recv()

        def s7():
            for name in ("a", "b0", "b1", "c"):
                st[name].wait_send()

            @pl.when(mid)
            def _():
                st["z2"].wait_send()
                st["z3"].wait_send()

            @pl.when(jnp.logical_not(mid))
            def _():
                st["z1"].wait_send()

        return [s0, s1, s2, s3, s4, s5, s6, s7]

    pieces = []
    for a in (1, 0):
        half = big[a][2].shape[1]
        for k in range(6):
            pieces.append(piece(a, k, half // 6, k % 2 == 0))
    pieces.insert(1, small_piece())
    greet([(core_r, s), (rep, x_s), (rep, y_s), (pair_r, s), (mid_r, s)])
    early = 7
    for p in pieces[:early]:
        p[0]()
    turned[...] = jnp.transpose(normed_ref[...].astype(F32)).astype(BF)
    columns = gp_ref.shape[1]
    per = gin_ref.shape[1]
    tile = 4 * LANES
    tiles = list(range(0, columns, tile))

    def grad_tile(lo):
        hi = min(lo + tile, columns)
        value = dot(turned[...], gp_ref[:, lo:hi]).astype(BF)
        for k in range(n):
            gin_ref[k, :, lo:hi] = value[k * per : (k + 1) * per, :]

    total = len(pieces)
    for t in range(total + lead[-1]):
        for stage, lag in enumerate(lead):
            k = t - lag
            if 0 <= k < total:
                pieces[k][stage + 1]()
        for lo in tiles[2 * t : 2 * t + 2]:
            grad_tile(lo)
        if 2 * t < len(tiles) <= 2 * t + 2:
            for p in pieces[early:]:
                p[0]()
    for p in pieces:
        p[7]()


def reduce_call(normed, grad_proj, g_out, dpar, dhead, n, dims):
    cw, gw, nw, hw = dims
    wide = -(-max(cw, 3 * LANES) // LANES) * LANES
    depth, w_in = normed.shape[1], grad_proj.shape[1]
    h_in = depth // n // 2
    h_out, w_out = g_out.shape[0] // n // 2, g_out.shape[1]
    sds = jax.ShapeDtypeStruct
    vm = pl.BlockSpec(memory_space=pltpu.VMEM)
    both = lambda lead: [pltpu.VMEM((*lead, h_in, w_in), BF), pltpu.VMEM((*lead, h_out, w_out), BF)]
    sm = lambda k: pltpu.VMEM((k, 8, wide), F32)
    copies = 13 * 10
    fin, fout, fs = pl.pallas_call(
        functools.partial(reduce_kernel, dims, (0, 2, 4, 6, 8, 10)),
        in_specs=[vm] * 5,
        out_specs=[vm] * 3,
        out_shape=[sds((2, h_in, w_in), BF), sds((2, h_out, w_out), BF), sds((8, wide), F32)],
        scratch_shapes=[
            *both((n,)), sm(n), *both((2,)), sm(3), *both(()), pltpu.VMEM((8, wide), F32),
            *both((2,)), sm(2 + n), *both(()),
            pltpu.VMEM((n, 2 * h_in, w_in), BF), pltpu.VMEM((depth, normed.shape[0]), BF),
            pltpu.SemaphoreType.DMA((copies,)), pltpu.SemaphoreType.DMA((copies,)),
        ],
        compiler_params=pltpu.CompilerParams(
            collective_id=1, has_side_effects=True, vmem_limit_bytes=56 * 1024 * 1024
        ),
    )(normed, grad_proj, g_out.reshape(n, 2 * h_out, w_out), dpar, dhead)
    return fin.reshape(-1, w_in).astype(F32), fout.reshape(-1, w_out).astype(F32), fs


def pack_small(shards, wide):
    taps, bias, step, decay, skip, norm, gate = [p.astype(F32) for p in shards]
    taps_n = taps.shape[0]
    put = lambda v, row, lane: jnp.pad(
        v, ((row, 8 - row - v.shape[0]), (lane, wide - lane - v.shape[1]))
    )
    return (
        put(taps, 0, 0) + put(bias[None], taps_n, 0) + put(gate[None], 5, 0) + put(norm[None], 6, 0)
        + put(step[None], 7, 0) + put(decay[None], 7, LANES) + put(skip[None], 7, 2 * LANES)
    )


def on_device(tokens, cotangent, doc_lengths, *shards):
    n, chips = lax.axis_size("shard"), lax.axis_size("replica") // 2
    me, rep = lax.axis_index("shard"), lax.axis_index("replica")
    core, chip = lax.rem(rep, 2), lax.div(rep, 2)
    cw, gw, nw, hw = shards[2].shape[1], shards[8].shape[0], shards[7].shape[0], shards[4].shape[0]
    dims = (cw, gw, nw, hw)
    wide = -(-max(cw, gw, nw, 3 * LANES) // LANES) * LANES
    small = pack_small(shards[2:], wide)
    direct = n == 4 and chips == 4
    if direct:
        in_full, out_full, par, head = gather_call(shards[0], shards[1], small, n, dims)
    else:
        small_all = ring_all(small, me, n, shard_step)
        out_full = gather_weight(shards[1], core, me, n)
        in_full = gather_weight(shards[0], core, me, n)
        total = n * cw
        row = lambda r0, r1, w, at: jnp.pad(
            small_all[:, r0:r1, at : at + w].transpose(1, 0, 2).reshape(r1 - r0, n * w),
            ((0, 0), (0, total - n * w)),
        )
        heads = [row(7, 8, hw, k * LANES) for k in range(3)]
        skip_row = jnp.pad(jnp.repeat(heads[2][:, : n * hw], gw // hw, axis=1), ((0, 0), (0, total - n * gw)))
        par = jnp.concatenate([row(0, 5, cw, 0), row(5, 6, gw, 0), row(6, 7, nw, 0), skip_row])
        head = jnp.pad(jnp.concatenate([h[:, :LANES] for h in heads]), ((0, 5), (0, 0)))
    layer, input_grad, normed, grad_proj, grad_out, dpar, dhead = device_part(
        tokens, cotangent, doc_lengths, in_full, out_full, par, head, n, dims
    )
    if direct:
        big_in, big_out, mine = reduce_call(normed, grad_proj, grad_out.astype(BF), dpar, dhead, n, dims)
    else:
        blocks = []
        for k in range(n):
            fit = lambda v, w: jnp.pad(v[:, k * w : (k + 1) * w], ((0, 0), (0, wide - w)))
            last = [jnp.pad(dhead[j : j + 1, k * hw : (k + 1) * hw], ((0, 0), (0, LANES - hw))) for j in range(3)]
            last = jnp.concatenate(last, axis=1)
            blocks.append(jnp.concatenate([
                fit(dpar[:5], cw), fit(dpar[5:6], gw), fit(dpar[6:7], nw),
                jnp.pad(last, ((0, 0), (0, wide - 3 * LANES))),
            ]).reshape(-1, LANES))
        unit = 2 * chips * 8
        packed = jnp.stack(blocks)
        size = packed.shape[1]
        packed = jnp.pad(packed, ((0, 0), (0, -size % unit), (0, 0))).reshape(-1, LANES)
        reduce = functools.partial(reduce_grad, core=core, me=me, n=n, chip=chip, chips=chips)
        big_out = reduce(grad_out, kind=BF)
        big_in = reduce(dot(normed, grad_proj, ((0,), (0,))), kind=BF)
        mine = reduce(packed, kind=F32)[:size].reshape(8, wide)
    outs = [
        mine[0:4, :cw], mine[4, :cw], mine[7, :hw], mine[7, LANES : LANES + hw],
        mine[7, 2 * LANES : 2 * LANES + hw], mine[6, :nw], mine[5, :gw],
    ]
    return (layer, input_grad, big_in, big_out, *outs)


def solution(mesh):
    tok = P(("replica", "shard"), None)
    weights = (P("shard", None), P("shard", None), P(None, "shard")) + (P("shard"),) * 6
    return jax.shard_map(
        on_device,
        mesh=mesh,
        in_specs=(tok, tok, tok) + weights,
        out_specs=(tok, tok) + weights,
        check_vma=False,
    )
```
